512 devices in a mesh: ctx: 64 (over y, z), tp: 8 (over x, core).
Axes of the slice: x: 4, y: 8, z: 8, core: 2. Of those that a mesh axis runs over, the one named last changes fastest.
Arguments:
- tokens: bfloat16 [8192, 4096], P('ctx', 'tp'), may hold values from -216 to 216
- norm_gain: float32 [4096], P('tp'), may hold values from 0.5 to 1.5
- norm_bias: float32 [4096], P('tp'), may hold values from -3 to 3
- ema_decay: float32 [16, 4096], P(None, 'tp'), may hold values from 0.96 to 1
- ema_phase: float32 [16, 4096], P(None, 'tp'), may hold values from -1 to 1
- ema_in: float32 [16, 4096], P(None, 'tp'), may hold values from -0.6 to 0.6
- ema_out: float32 [2, 16, 4096], P(None, None, 'tp'), may hold values from -1.5 to 1.5
- ema_skip: float32 [4096], P('tp'), may hold values from -4 to 4
- rms_gain: float32 [4096], replicated, may hold values from 0.5 to 1.5
- z_weight: bfloat16 [4096, 1024], P('ctx', 'tp'), may hold values from -0.09375 to 0.09375
- v_weight: bfloat16 [4096, 8192], P('ctx', 'tp'), may hold values from -0.09375 to 0.09375
- qk_affine: float32 [4, 1024], P(None, 'tp'), may hold values from -1.5 to 4, as said below
Outputs:
- attended: bfloat16 [8192, 8192], P('ctx', 'tp')
The draws below stay inside these ranges and needn't reach their ends.
Inputs may be any that keep to these rules, and one draw needn't show every extreme that they name: `qk_affine`: rows 0 and 2 are positive.
All inputs are finite; a program needn't handle non-finite values.
Results may differ from the reference program's by a relative error of at most 0.015.
The reference program's roundings to bfloat16 on the way (of `normed`, `mixed_rows`, `rms_normed` and `probabilities`) count: a program that leaves them out, or rounds other values in their place, can miss the bound.
Values may be sent and summed in bfloat16 or wider, within the bound.
A program may use at most 64 MiB of HBM per device.

```python
import math
import jax
import jax.numpy as jnp
from jax import lax

D = 4096
NDIM = 16
ZH = 128
VH = 1024
GROUP = 64
STRETCH = 128
EBLK = 32
TOKENS = 8192
ZDIM = 1024
VDIM = 8192


def draw_tokens(key, part):
    keys = jax.random.split(key, 4)
    block_count = TOKENS // EBLK
    base = jax.random.truncated_normal(keys[0], -6.0, 6.0, (TOKENS, D), jnp.float32)
    shifts = jnp.repeat(jax.random.uniform(keys[1], (block_count, D), jnp.float32, -1.0, 1.0), EBLK, axis=0)
    row_scale = jnp.repeat(jnp.exp(jax.random.uniform(keys[2], (block_count, 1), jnp.float32, 0.0, math.log(3.2))), EBLK, axis=0)
    column_scale = jnp.exp(jax.random.uniform(keys[3], (1, D), jnp.float32, 0.0, math.log(3.2)))
    ramp = jnp.exp(math.log(3.0) * jnp.arange(TOKENS, dtype=jnp.float32) / TOKENS)[:, None]
    return ((base + shifts) * row_scale * column_scale * ramp).astype(jnp.bfloat16)


def draw_ema_decay(key, part):
    keys = jax.random.split(key, 3)
    slow_share = 0.5
    slower = jax.random.bernoulli(keys[0], slow_share, (NDIM, D))
    fast_rate = jnp.exp(jax.random.uniform(keys[1], (NDIM, D), jnp.float32, math.log(1.0 / 50.0), math.log(1.0 / 30.0)))
    slow_rate = jax.random.uniform(keys[2], (NDIM, D), jnp.float32, 0.1, 2.0) / TOKENS
    return jnp.exp(-jnp.where(slower, slow_rate, fast_rate)).astype(jnp.float32)


def draw_qk_affine(key, part):
    keys = jax.random.split(key, 4)
    gain_low, gain_high = (math.log(0.5), math.log(2.0))
    query_gain = jnp.exp(jax.random.uniform(keys[0], (ZDIM,), jnp.float32, gain_low, gain_high))
    key_gain = jnp.exp(jax.random.uniform(keys[1], (ZDIM,), jnp.float32, gain_low, gain_high))
    query_bias = 0.3 * jax.random.truncated_normal(keys[2], -5.0, 5.0, (ZDIM,), jnp.float32)
    key_bias = 0.3 * jax.random.truncated_normal(keys[3], -5.0, 5.0, (ZDIM,), jnp.float32)
    return jnp.stack([query_gain, query_bias, key_gain, key_bias]).astype(jnp.float32)


def steps_of(own_key, shape, cuts, low, top_value):
    def one(axis_at, shards_of):
        draws = jax.random.uniform(jax.random.fold_in(jax.random.fold_in(own_key, 6), axis_at), (shards_of,), jnp.float32, low / len(cuts), top_value / len(cuts))
        return jnp.repeat(jnp.exp(draws), shape[axis_at] // shards_of).reshape((-1,) + (1,) * (len(shape) - axis_at - 1))

    factor_of = one(*cuts[0])
    for cut in cuts[1:]:
        factor_of = factor_of * one(*cut)
    return factor_of


def normal_values(own_key, shape, deviation, limit, pieces=(), kind=jnp.bfloat16):
    level = steps_of(own_key, shape, pieces, -0.22, 0.18) if pieces else 1.0
    values = jax.random.normal(own_key, shape, jnp.float32) * deviation * level
    return jnp.minimum(jnp.maximum(values, -limit), limit).astype(kind)


def setup_inputs(seed: int = 0) -> dict:
    key_list = jax.random.split(jax.random.key(seed), 13)
    return {
        "tokens": draw_tokens(jax.random.fold_in(key_list[12], 71), 0),
        "norm_gain": jnp.clip(1.0 + 0.1 * jax.random.normal(key_list[1], (D,), jnp.float32), 0.5, 1.5),
        "norm_bias": normal_values(key_list[2], (D,), 0.5, 3.0, ((0, 8),), jnp.float32),
        "ema_decay": draw_ema_decay(jax.random.fold_in(key_list[12], 71), 0),
        "ema_phase": jnp.clip(jax.random.uniform(key_list[4], (NDIM, D), jnp.float32, -1.0, 1.0) * steps_of(key_list[4], (NDIM, D), ((1, 8),), -0.4, 0.0), -1.0, 1.0),
        "ema_in": normal_values(key_list[5], (NDIM, D), 0.1, 0.6, ((1, 8),), jnp.float32),
        "ema_out": normal_values(key_list[6], (2, NDIM, D), NDIM ** -0.5, 1.5, ((2, 8),), jnp.float32),
        "ema_skip": normal_values(key_list[7], (D,), 1.0, 4.0, ((0, 8),), jnp.float32),
        "rms_gain": jnp.clip(1.0 + 0.1 * jax.random.normal(key_list[8], (D,), jnp.float32), 0.5, 1.5),
        "z_weight": normal_values(key_list[9], (D, ZDIM), D ** -0.5, 0.09375, ((0, 64), (1, 8))),
        "v_weight": normal_values(key_list[10], (D, VDIM), D ** -0.5, 0.09375, ((0, 64), (1, 8))),
        "qk_affine": draw_qk_affine(jax.random.fold_in(key_list[12], 71), 0),
    }


highest = lax.Precision.HIGHEST
epsilon = 1e-05

def ema_tables(decays, phases, ema_in, ema_out, blocklen):
    log_rate = jnp.log(decays)
    powers = jnp.arange(blocklen + 1, dtype=jnp.float32)[:, None, None]
    magnitude = jnp.exp(powers * log_rate)
    power_re = magnitude * jnp.cos(powers * phases)
    power_im = magnitude * jnp.sin(powers * phases)
    coef_re = ema_out[0] * power_re - ema_out[1] * power_im
    coef_im = ema_out[0] * power_im + ema_out[1] * power_re
    kernel = lax.optimization_barrier(jnp.sum(ema_in * coef_re[:blocklen], axis=1))
    offsets = jnp.arange(blocklen)[:, None] - jnp.arange(blocklen)[None, :]
    toeplitz = jnp.where((offsets >= 0)[:, :, None], kernel[jnp.clip(offsets, 0, blocklen - 1)], 0.0)
    feed_re = ema_in * power_re[::-1][1:]
    feed_im = ema_in * power_im[::-1][1:]
    return (toeplitz, coef_re[1:], coef_im[1:], feed_re, feed_im, power_re[blocklen], power_im[blocklen])

def ema_feed(tables, inputs):
    fresh_re = jnp.einsum('sc,sjc->jc', inputs, tables[3], precision=highest)
    fresh_im = jnp.einsum('sc,sjc->jc', inputs, tables[4], precision=highest)
    return (fresh_re, fresh_im)

def rotate(tables, hidden_state, inputs):
    state_re, state_im = hidden_state
    fresh_re, fresh_im = ema_feed(tables, inputs)
    new_re = tables[5] * state_re - tables[6] * state_im + fresh_re
    new_im = tables[5] * state_im + tables[6] * state_re + fresh_im
    return (new_re, new_im)

def ema_block(tables, hidden_state, inputs):
    state_re, state_im = hidden_state
    within = jnp.einsum('tsc,sc->tc', tables[0], inputs, precision=highest)
    carried = jnp.einsum('tjc,jc->tc', tables[1], state_re, precision=highest) - jnp.einsum('tjc,jc->tc', tables[2], state_im, precision=highest)
    return (rotate(tables, hidden_state, inputs), within + carried)

def attention(z_total, v_total, affine):
    queries = (z_total * affine[0] + affine[1]).astype(jnp.bfloat16)
    key_rows = (z_total * affine[2] + affine[3]).astype(jnp.bfloat16)
    values = jax.nn.silu(v_total).astype(jnp.bfloat16)
    row_count = z_total.shape[0]
    stretches = row_count // STRETCH
    queries = queries.reshape(stretches, STRETCH, -1).astype(jnp.float32)
    key_rows = key_rows.reshape(stretches, STRETCH, -1).astype(jnp.float32)
    values = values.reshape(stretches, STRETCH, -1).astype(jnp.float32)
    scores = jnp.einsum('nqd,nkd->nqk', queries, key_rows) * (1.0 / ZH ** 0.5)
    causal = jnp.arange(STRETCH)[:, None] >= jnp.arange(STRETCH)[None, :]
    scores = jnp.where(causal[None], scores, -1e+30)
    row_max = lax.optimization_barrier(jnp.max(scores, axis=-1, keepdims=True))
    weights = jnp.exp(scores - row_max)
    probabilities = (weights / lax.optimization_barrier(jnp.sum(weights, axis=-1, keepdims=True))).astype(jnp.bfloat16)
    result = jnp.einsum('nqk,nkd->nqd', probabilities.astype(jnp.float32), values)
    return result.reshape(row_count, -1).astype(jnp.bfloat16)

def reference(tokens, norm_gain, norm_bias, ema_decay, ema_phase, ema_in, ema_out, ema_skip, rms_gain, z_weight, v_weight, qk_affine):
    length = tokens.shape[0]
    model_width = tokens.shape[1]
    groups = model_width // GROUP
    x_float = tokens.astype(jnp.float32).reshape(length, groups, GROUP)
    prefix_sums = jnp.cumsum(lax.optimization_barrier(jnp.sum(x_float, axis=-1)), axis=0)
    prefix_squares = jnp.cumsum(lax.optimization_barrier(jnp.sum(x_float * x_float, axis=-1)), axis=0)
    counts = (jnp.arange(length, dtype=jnp.float32)[:, None] + 1.0) * GROUP
    average = prefix_sums / counts
    spread = jnp.maximum(prefix_squares / counts - average * average, 0.0)
    scaled = (x_float - average[..., None]) * lax.rsqrt(spread + epsilon)[..., None]
    normed = (scaled.reshape(length, model_width) * norm_gain + norm_bias).astype(jnp.bfloat16)
    inputs = normed.astype(jnp.float32)
    tables = ema_tables(ema_decay, ema_phase, ema_in, ema_out, EBLK)

    def advance(hidden_state, block_rows):
        return ema_block(tables, hidden_state, block_rows)
    initial = (jnp.zeros((NDIM, model_width), jnp.float32), jnp.zeros((NDIM, model_width), jnp.float32))
    _, outputs = lax.scan(advance, initial, inputs.reshape(length // EBLK, EBLK, model_width))
    mixed_rows = jax.nn.silu(outputs.reshape(length, model_width) + ema_skip * inputs).astype(jnp.bfloat16)
    mixed_float = mixed_rows.astype(jnp.float32)
    rms_normed = (mixed_float * lax.rsqrt(lax.optimization_barrier(jnp.mean(mixed_float * mixed_float, axis=-1, keepdims=True)) + 1e-06) * rms_gain).astype(jnp.bfloat16)
    head_count = z_weight.shape[1] // ZH

    def one_head(head_index):
        z_columns = lax.dynamic_slice_in_dim(z_weight, head_index * ZH, ZH, 1)
        v_columns = lax.dynamic_slice_in_dim(v_weight, head_index * VH, VH, 1)
        affine = lax.dynamic_slice_in_dim(qk_affine, head_index * ZH, ZH, 1)
        z_total = jnp.dot(rms_normed, z_columns, preferred_element_type=jnp.float32)
        v_total = jnp.dot(normed, v_columns, preferred_element_type=jnp.float32)
        return attention(z_total, v_total, affine)
    stacked = lax.map(one_head, jnp.arange(head_count))
    return stacked.transpose(1, 0, 2).reshape(length, head_count * VH)
```

```python
import functools
import math

import jax
import jax.numpy as jnp
from jax import lax
from jax.experimental import pallas as pl
from jax.experimental.pallas import tpu as pltpu
from jax.sharding import PartitionSpec as P

NDIM = 16
ZH = 128
GROUP = 64
STRETCH = 128
SUB = 8
LANES = 128
DEPTH = 2
MESH = pl.DeviceIdType.MESH
f32 = jnp.float32
bf16 = jnp.bfloat16
highest = lax.Precision.HIGHEST


def link_lists(Y, Z):
    def reach(n, extra_plus):
        return (n // 2, (n - 1) // 2) if extra_plus else ((n - 1) // 2, n // 2)

    def arrival(n, extra_plus):
        p, m = reach(n, extra_plus)
        order = [0]
        for d in range(1, max(p, m) + 1):
            if d <= p:
                order.append(-d)
            if d <= m:
                order.append(d)
        return order

    def spread(first, second, extra):
        fp, fm = reach(first, extra)
        early_p = [(-e, 0) for e in range(fp)]
        early_m = [(e, 0) for e in range(fm)]
        late_p, late_m = [], []
        order = arrival(first, extra)
        for e in range(second // 2 + 1):
            for i, o in enumerate(order):
                p, m = reach(second, i % 2 == 0)
                if e < p:
                    late_p.append((o, -e))
                if e < m:
                    late_m.append((o, e))
        return early_p, early_m, late_p, late_m

    zp, zm, yp2, ym2 = spread(Z, Y, True)
    yp, ym, zp2, zm2 = spread(Y, Z, False)

    def merge(early, late):
        early, late, both = list(early), list(late), []
        while early or late:
            if early:
                both.append(early.pop(0))
            if late:
                both.append(late.pop(0))
        return both

    A = lambda t: [(0, b, a) for a, b in t]
    B = lambda t: [(1, a, b) for a, b in t]
    return {
        "z+": merge(A(zp), B(zp2)),
        "z-": merge(A(zm), B(zm2)),
        "y+": merge(B(yp), A(yp2)),
        "y-": merge(B(ym), A(ym2)),
    }


DIRS = ("z+", "z-", "y+", "y-")
STEP = {"z+": (0, 1), "z-": (0, -1), "y+": (1, 0), "y-": (-1, 0)}


def silu(v):
    return v * (1.0 / (1.0 + jnp.exp(-v)))


def cmul(ar, ai, br, bi):
    return ar * br - ai * bi, ar * bi + ai * br


def sin_cos(p):
    s = p * p
    sine = p * (1.0 + s * (-1 / 6 + s * (1 / 120 + s * (-1 / 5040 + s * (1 / 362880 - s / 39916800)))))
    cosine = 1.0 + s * (
        -0.5 + s * (1 / 24 + s * (-1 / 720 + s * (1 / 40320 + s * (-1 / 3628800 + s / 479001600))))
    )
    return sine, cosine


def kernel(
    Y, Z, X, plan,
    tok, gain, bias, decay, phase, e_in, e_out, skip, rgain, zw, vw, affine,
    out,
    W, NF, MF, N32, TB, LOC, PW, QP, QX, TOT, RS, CS, OUTS, IS, S1, S2, ACC, HID,
    wsend, wrecv, lsem, ssend, srecv, tsend, trecv,
):
    ctx, tp = lax.axis_index("ctx"), lax.axis_index("tp")
    y, z = ctx // Z, ctx % Z
    x, core = tp // 2, tp % 2
    T, L, CL = NF.shape
    KR = W.shape[1]
    VC = vw.shape[1]
    JS = NDIM // Z
    tiles = CL // LANES
    sib = x * 2 + (1 - core)

    def at(dy, dz):
        return lax.rem(y + dy + Y, Y) * Z + lax.rem(z + dz + Z, Z)

    load_v = pltpu.make_async_copy(vw, W.at[ctx, :, pl.ds(0, VC)], lsem.at[0])
    load_z = pltpu.make_async_copy(zw, W.at[ctx, :, pl.ds(VC, ZH)], lsem.at[1])
    load_v.start()
    load_z.start()

    barrier = pltpu.get_barrier_semaphore()
    peers = [(y * Z + lax.rem(z + d, Z), tp) for d in range(1, Z)]
    peers += [(lax.rem(y + d, Y) * Z + z, tp) for d in range(1, Y)]
    peers += [(ctx, lax.rem(x + d, X) * 2 + core) for d in range(1, X)]
    peers += [(ctx, sib)]
    for peer in peers:
        pl.semaphore_signal(barrier, inc=1, device_id=peer, device_id_type=MESH)

    xb = tok[...]
    xf = xb.astype(f32)
    same = (
        lax.broadcasted_iota(jnp.int32, (CL, CL), 0) // GROUP
        == lax.broadcasted_iota(jnp.int32, (CL, CL), 1) // GROUP
    )
    same = jnp.where(same, 1.0, 0.0).astype(bf16)
    sq = xf * xf
    sq_hi = sq.astype(bf16)
    sq_lo = (sq - sq_hi.astype(f32)).astype(bf16)
    dot = functools.partial(jnp.dot, preferred_element_type=f32)
    row_sums = dot(xb, same)
    row_squares = dot(sq_hi, same) + dot(sq_lo, same)
    lower = jnp.where(
        lax.broadcasted_iota(jnp.int32, (L, L), 0) >= lax.broadcasted_iota(jnp.int32, (L, L), 1), 1.0, 0.0
    ).astype(f32)
    run_sums = dot(lower, row_sums, precision=highest)
    run_squares = dot(lower, row_squares, precision=highest)
    HID[0] = run_sums
    HID[1] = run_squares
    S1[z, 0:1] = run_sums[L - 1 : L]
    S1[z, 1:2] = run_squares[L - 1 : L]

    pl.semaphore_wait(barrier, len(peers))

    def row_peer(d):
        z2 = lax.rem(z + d, Z)
        return z2, (y * Z + z2, tp)

    def col_peer(d):
        y2 = lax.rem(y + d, Y)
        return y2, (y2 * Z + z, tp)

    def exchange(phase_at, n, mine, peer_of, source, dest):
        copies = []
        for d in range(1, n):
            who, dev = peer_of(d)
            c = pltpu.make_async_remote_copy(
                src_ref=source.at[who] if source is not dest else source.at[mine],
                dst_ref=dest.at[mine],
                send_sem=ssend.at[phase_at, d - 1],
                recv_sem=srecv.at[phase_at, d - 1],
                device_id=dev,
                device_id_type=MESH,
            )
            c.start()
            copies.append(c)

        def finish():
            for c in copies:
                c.wait_recv()
            for c in copies:
                c.wait_send()

        return finish

    half = KR // 2
    state = {"slot": 0, "waited": set()}

    def piece(h, oy, oz):
        src = at(oy, oz)
        return src, W.at[src, pl.ds(h * half, half), :]

    def await_piece(h, oy, oz):
        if (oy, oz) == (0, 0) or (h, oy % Y, oz % Z) in state["waited"]:
            return
        state["waited"].add((h, oy % Y, oz % Z))
        src, ref = piece(h, oy, oz)
        pltpu.make_async_remote_copy(
            src_ref=ref, dst_ref=ref, send_sem=wsend.at[0, 0], recv_sem=wrecv.at[h, src],
            device_id=(at(0, 1), tp), device_id_type=MESH,
        ).wait_recv()

    def send_piece(k, i, start):
        h, oy, oz = plan[DIRS[k]][i]
        src, ref = piece(h, oy, oz)
        c = pltpu.make_async_remote_copy(
            src_ref=ref, dst_ref=ref, send_sem=wsend.at[k, i % DEPTH], recv_sem=wrecv.at[h, src],
            device_id=(at(*STEP[DIRS[k]]), tp), device_id_type=MESH,
        )
        if start:
            c.start()
        else:
            c.wait_send()

    slots = max(len(plan[d]) for d in DIRS)

    def pump(n):
        for _ in range(n):
            i = state["slot"]
            if i >= slots:
                return
            for k, d in enumerate(DIRS):
                if i < len(plan[d]):
                    await_piece(*plan[d][i])
                    if i >= DEPTH:
                        send_piece(k, i - DEPTH, False)
                    send_piece(k, i, True)
            state["slot"] = i + 1

    def drain():
        pump(slots)
        for k, d in enumerate(DIRS):
            n = len(plan[d])
            for i in range(max(n - DEPTH, 0), n):
                send_piece(k, i, False)
        for h in range(2):
            for oy in range(Y):
                for oz in range(Z):
                    await_piece(h, oy, oz)

    stats_row = exchange(0, Z, z, row_peer, S1, S1)
    load_v.wait()
    load_z.wait()
    pump(1)

    sine, cosine = sin_cos(phase[...])
    dec = decay[...]
    qr, qi = dec * cosine, dec * sine
    QP[0], QP[1] = qr, qi
    ein = e_in[...]
    QP[2], QP[3] = ein * e_out[0], ein * e_out[1]
    pr, pi = qr, qi
    for k in range(1, 11):
        pr, pi = cmul(pr, pi, pr, pi)
        if k in (4, 5, 6):
            QP[2 * k - 4], QP[2 * k - 3] = pr, pi
        if k == 7:
            q7 = (pr, pi)
        if 2**k == STRETCH * Z:
            q10 = (pr, pi)
    for s in range(Z):
        for r, part in enumerate((*q7, *q10)):
            QX[s, r] = part[s * JS : (s + 1) * JS]
    for t in range(4):
        for j in range(NDIM):
            TB[t, j] = jnp.broadcast_to(QP[t, j : j + 1], (SUB, CL))

    stats_row()
    before, whole = jnp.zeros((2, CL), f32), jnp.zeros((2, CL), f32)
    for k in range(Z):
        part = S1[k]
        before = before + jnp.where(k < z, part, 0.0)
        whole = whole + part
    S2[y] = whole
    stats_col = exchange(1, Y, y, col_peer, S2, S2)
    pump(2)
    sub_row = lax.broadcasted_iota(jnp.int32, (SUB, LANES), 0)
    stats_col()
    for k in range(Y):
        before = before + jnp.where(k < y, S2[k], 0.0)
    counts = ((ctx * L + lax.broadcasted_iota(jnp.int32, (L, 1), 0)) + 1).astype(f32) * GROUP
    average = (before[0:1] + HID[0]) / counts
    spread = jnp.maximum((before[1:2] + HID[1]) / counts - average * average, 0.0)
    scaled = (tok[...].astype(f32) - average) * lax.rsqrt(spread + 1e-5)
    normed = (scaled * gain[...] + bias[...]).astype(bf16)
    NF[tp] = normed
    for t in range(tiles):
        N32[t] = normed[:, t * LANES : (t + 1) * LANES].astype(f32)

    def share(base, buf):
        def copy(block, dev, k):
            return pltpu.make_async_remote_copy(
                src_ref=buf.at[block], dst_ref=buf.at[block],
                send_sem=tsend.at[base + k], recv_sem=trecv.at[base + k],
                device_id=(ctx, dev), device_id_type=MESH,
            )

        direct = [copy(tp, lax.rem(x + d, X) * 2 + core, d - 1) for d in range(1, X)]
        other = copy(tp, sib, X - 1)
        for c in direct:
            c.start()
        other.start()
        relays = []

        def relay():
            for d in range(1, X):
                block = lax.rem(x - d + X, X) * 2 + core
                copy(block, sib, d - 1).wait_recv()
                c = copy(block, sib, X - 1 + d)
                c.start()
                relays.append(c)

        def finish():
            copy(sib, sib, X - 1).wait_recv()
            for d in range(1, X):
                copy(lax.rem(x - d + X, X) * 2 + 1 - core, sib, X - 1 + d).wait_recv()
            for c in (*direct, other, *relays):
                c.wait_send()

        return relay, finish

    normed_relay, normed_done = share(0, NF)

    per = L // SUB

    def first_pass(t):
        cs = pl.ds(t * LANES, LANES)

        def step(i, st):
            v = N32[t, pl.ds(i, SUB, stride=per)]
            new = []
            for j in range(NDIM):
                sr, si = st[2 * j], st[2 * j + 1]
                a, b = TB[0, j, :, cs], TB[1, j, :, cs]
                new += [a * sr - b * si + v, a * si + b * sr]
            return tuple(new)

        zero = jnp.zeros((SUB, LANES), f32)
        st = lax.fori_loop(0, per, step, (zero,) * (2 * NDIM))
        for j in range(NDIM):
            ir, ii = st[2 * j], st[2 * j + 1]
            for n, sh in enumerate((1, 2, 4)):
                fr, fi = QP[4 + 2 * n, j : j + 1, cs], QP[5 + 2 * n, j : j + 1, cs]
                rr, ri = pltpu.roll(ir, sh, 0), pltpu.roll(ii, sh, 0)
                mr, mi = cmul(fr, fi, rr, ri)
                keep = sub_row >= sh
                ir, ii = ir + jnp.where(keep, mr, 0.0), ii + jnp.where(keep, mi, 0.0)
            TOT[j // JS, j % JS : j % JS + 1, cs] = ir[SUB - 1 : SUB]
            TOT[j // JS, JS + j % JS : JS + j % JS + 1, cs] = ii[SUB - 1 : SUB]
            LOC[j, 0, :, cs] = jnp.where(sub_row >= 1, pltpu.roll(ir, 1, 0), 0.0)
            LOC[j, 1, :, cs] = jnp.where(sub_row >= 1, pltpu.roll(ii, 1, 0), 0.0)

    def sub_powers(t):
        cs = pl.ds(t * LANES, LANES)
        for j in range(NDIM):
            wr, wi = jnp.ones((SUB, LANES), f32), jnp.zeros((SUB, LANES), f32)
            for n, bit in enumerate((1, 2, 4)):
                fr, fi = QP[4 + 2 * n, j : j + 1, cs], QP[5 + 2 * n, j : j + 1, cs]
                mr, mi = cmul(wr, wi, fr, fi)
                on = (sub_row // bit) % 2 == 1
                wr, wi = jnp.where(on, mr, wr), jnp.where(on, mi, wi)
            PW[j, 0, :, cs], PW[j, 1, :, cs] = wr, wi

    for t in range(tiles):
        first_pass(t)
        pump(1)

    RS[z] = TOT[z]
    states_row = exchange(2, Z, z, row_peer, TOT, RS)
    normed_relay()
    for t in range(tiles):
        sub_powers(t)
    pump(2)
    states_row()
    q128r, q128i, q1kr, q1ki = QX[z, 0], QX[z, 1], QX[z, 2], QX[z, 3]

    def onward(sr, si, fr, fi, part):
        nr, ni = cmul(sr, si, fr, fi)
        return nr + part[0:JS], ni + part[JS : 2 * JS]

    sr, si = jnp.zeros((JS, CL), f32), jnp.zeros((JS, CL), f32)
    for k in range(Z):
        sr, si = onward(sr, si, q128r, q128i, RS[k])
    CS[y, 0:JS], CS[y, JS : 2 * JS] = sr, si
    states_col = exchange(3, Y, y, col_peer, CS, CS)
    pump(2)
    normed_done()
    states_col()
    sr, si = jnp.zeros((JS, CL), f32), jnp.zeros((JS, CL), f32)
    for k in range(Y):
        nr, ni = onward(sr, si, q1kr, q1ki, CS[k])
        sr, si = jnp.where(k < y, nr, sr), jnp.where(k < y, ni, si)
    for k in range(Z):
        OUTS[k, 0:JS], OUTS[k, JS : 2 * JS] = sr, si
        if k + 1 < Z:
            sr, si = onward(sr, si, q128r, q128i, RS[k])
    IS[z] = OUTS[z]
    states_back = exchange(4, Z, z, row_peer, OUTS, IS)
    pump(3)
    states_back()

    def second_pass(t):
        cs = pl.ds(t * LANES, LANES)
        init = []
        for j in range(NDIM):
            gr = IS[j // JS, j % JS : j % JS + 1, cs]
            gi = IS[j // JS, JS + j % JS : JS + j % JS + 1, cs]
            mr, mi = cmul(PW[j, 0, :, cs], PW[j, 1, :, cs], gr, gi)
            init += [LOC[j, 0, :, cs] + mr, LOC[j, 1, :, cs] + mi]
        sk = skip[:, cs]

        def step(i, st):
            v = N32[t, pl.ds(i, SUB, stride=per)]
            new, total = [], sk * v
            for j in range(NDIM):
                sr, si = st[2 * j], st[2 * j + 1]
                a, b = TB[0, j, :, cs], TB[1, j, :, cs]
                nr, ni = a * sr - b * si + v, a * si + b * sr
                total = total + (TB[2, j, :, cs] * nr - TB[3, j, :, cs] * ni)
                new += [nr, ni]
            ACC[t, pl.ds(i, SUB, stride=per)] = total
            return tuple(new)

        lax.fori_loop(0, per, step, tuple(init))

    for t in range(tiles):
        second_pass(t)
        MF[tp, :, t * LANES : (t + 1) * LANES] = silu(ACC[t]).astype(bf16)
        pump(1)
    mixed_relay, mixed_done = share(2 * X, MF)
    pump(2)
    mixed_relay()
    pump(1)
    mixed_done()

    squares = jnp.zeros((L, CL), f32)
    for t in range(T):
        m = MF[t].astype(f32)
        squares = squares + m * m
    rinv = lax.rsqrt(jnp.sum(squares, axis=-1, keepdims=True) * (1.0 / (T * CL)) + 1e-6)
    for t in range(T):
        MF[t] = (MF[t].astype(f32) * rinv * rgain[:, t * CL : (t + 1) * CL]).astype(bf16)

    drain()

    per_block = W.shape[0] // T
    zero_z = jnp.zeros((L, ZH), f32)
    z_total = zero_z
    for t in range(T):
        wz = W[t * per_block : (t + 1) * per_block, :, VC : VC + ZH].reshape(CL, ZH)
        z_total = z_total + dot(MF[t], wz)
    queries = (z_total * affine[0:1] + affine[1:2]).astype(bf16)
    keys = (z_total * affine[2:3] + affine[3:4]).astype(bf16)
    scores = lax.dot_general(
        queries, keys, (((1,), (1,)), ((), ())), preferred_element_type=f32
    ) * (1.0 / ZH**0.5)
    causal = lax.broadcasted_iota(jnp.int32, (L, L), 0) >= lax.broadcasted_iota(jnp.int32, (L, L), 1)
    scores = jnp.where(causal, scores, -1e30)
    weights = jnp.exp(scores - jnp.max(scores, axis=-1, keepdims=True))
    probabilities = (weights / jnp.sum(weights, axis=-1, keepdims=True)).astype(bf16)

    width = min(VC, 256)

    @pl.loop(0, VC // width)
    def _(n):
        cols = pl.ds(pl.multiple_of(n * width, width), width)
        acc = jnp.zeros((L, width), f32)
        for t in range(T):
            wv = W[t * per_block : (t + 1) * per_block, :, cols].reshape(CL, width)
            acc = acc + dot(NF[t], wv)
        values = silu(acc).astype(bf16)
        out[:, cols] = dot(probabilities, values).astype(bf16)


def grid_of(mesh):
    n = mesh.shape["ctx"]
    rows = 1
    while rows * rows < n:
        rows *= 2
    return rows, n // rows


def solution(mesh):
    Y, Z = grid_of(mesh)
    T = mesh.shape["tp"]
    X = T // 2
    plan = link_lists(Y, Z)

    def body(tok, gain, bias, decay, phase, e_in, e_out, skip, rgain, zw, vw, affine):
        L, CL = tok.shape
        KR, VC = vw.shape
        JS = NDIM // Z
        row = lambda a: a.reshape(1, -1)
        vm = pl.BlockSpec(memory_space=pltpu.VMEM)
        hbm = pl.BlockSpec(memory_space=pl.ANY)
        V = pltpu.VMEM
        dma = pltpu.SemaphoreType.DMA
        most = max(Y, Z) - 1
        return pl.pallas_call(
            functools.partial(kernel, Y, Z, X, plan),
            out_shape=jax.ShapeDtypeStruct((L, VC), bf16),
            in_specs=[vm] * 9 + [hbm, hbm, vm],
            out_specs=vm,
            scratch_shapes=[
                V((Y * Z, KR, VC + ZH), bf16),
                V((T, L, CL), bf16),
                V((T, L, CL), bf16),
                V((CL // LANES, L, LANES), f32),
                V((4, NDIM, SUB, CL), f32),
                V((NDIM, 2, SUB, CL), f32),
                V((NDIM, 2, SUB, CL), f32),
                V((10, NDIM, CL), f32),
                V((Z, 4, JS, CL), f32),
                V((Z, 2 * JS, CL), f32),
                V((Z, 2 * JS, CL), f32),
                V((Y, 2 * JS, CL), f32),
                V((Z, 2 * JS, CL), f32),
                V((Z, 2 * JS, CL), f32),
                V((Z, 2, CL), f32),
                V((Y, 2, CL), f32),
                V((CL // LANES, L, LANES), f32),
                V((2, L, CL), f32),
                dma((4, DEPTH)),
                dma((2, Y * Z)),
                dma((2,)),
                dma((5, most)),
                dma((5, most)),
                dma((4 * X,)),
                dma((4 * X,)),
            ],
            compiler_params=pltpu.CompilerParams(
                collective_id=0, has_side_effects=True, vmem_limit_bytes=48 << 20
            ),
        )(tok, row(gain), row(bias), decay, phase, e_in, e_out, row(skip), row(rgain), zw, vw, affine)

    in_specs = (
        P("ctx", "tp"), P("tp"), P("tp"), P(None, "tp"), P(None, "tp"), P(None, "tp"), P(None, None, "tp"),
        P("tp"), P(), P("ctx", "tp"), P("ctx", "tp"), P(None, "tp"),
    )
    return jax.shard_map(body, mesh=mesh, in_specs=in_specs, out_specs=P("ctx", "tp"), check_vma=False)
```

```python
import functools
import math

import jax
import jax.numpy as jnp
from jax import lax
from jax.experimental import pallas as pl
from jax.experimental.pallas import tpu as pltpu
from jax.sharding import PartitionSpec as P

NDIM = 16
ZH = 128
GROUP = 64
STRETCH = 128
SUB = 8
LANES = 128
DEPTH = 2
MESH = pl.DeviceIdType.MESH
f32 = jnp.float32
bf16 = jnp.bfloat16
highest = lax.Precision.HIGHEST


def ring_lists(Y, Z):
    columns = [0]
    for d in range(1, Z // 2 + 1):
        columns += [-d] if 2 * d == Z else [-d, d]
    plus, minus = [], []
    for e in range(Y // 2 + 1):
        for i, oz in enumerate(columns):
            more, less = Y // 2, (Y - 1) // 2
            if e < (less if i % 2 else more):
                plus.append((oz, -e))
            if e < (more if i % 2 else less):
                minus.append((oz, e))
    return plus, minus


def silu(v):
    return v * (1.0 / (1.0 + jnp.exp(-v)))


def cmul(ar, ai, br, bi):
    return ar * br - ai * bi, ar * bi + ai * br


def sin_cos(p):
    s = p * p
    sine = p * (1.0 + s * (-1 / 6 + s * (1 / 120 + s * (-1 / 5040 + s * (1 / 362880 - s / 39916800)))))
    cosine = 1.0 + s * (
        -0.5 + s * (1 / 24 + s * (-1 / 720 + s * (1 / 40320 + s * (-1 / 3628800 + s / 479001600))))
    )
    return sine, cosine


def kernel(
    Y, Z, X, GS, plan,
    tok_h, gain_h, bias_h, decay_h, phase_h, e_in_h, e_out_h, skip_h, rgain_h, zw, vw, affine_h,
    out,
    tok, gain, bias, decay, phase, e_in, e_out, skip, rgain, affine,
    W, NF, MF, VB, VR, N32, TB, LOC, PW, QP, QX, TOT, RS, CS, OUTS, IS, S1, S2, ACC, HID,
    wsend, wrecv, zsend, zrecv, lsem, ssend, srecv, xsend, xrecv, gsend, grecv, vsend, vrecv,
):
    ctx, tp = lax.axis_index("ctx"), lax.axis_index("tp")
    y, z = ctx // Z, ctx % Z
    x, core = tp // 2, tp % 2
    group, r = z // GS, z % GS
    _, T, L, CL = NF.shape
    KR = W.shape[1]
    VC = vw.shape[1]
    VQ = VC // GS
    JS = NDIM // Z
    tiles = CL // LANES
    sib = x * 2 + (1 - core)
    right, left, far = (lax.rem(x + d, X) * 2 + core for d in (1, X - 1, X // 2))

    def at(dy, dz):
        return lax.rem(y + dy + Y, Y) * Z + lax.rem(z + dz + Z, Z)

    def remote(src, dst, send, recv, dev):
        return pltpu.make_async_remote_copy(
            src_ref=src, dst_ref=dst, send_sem=send, recv_sem=recv, device_id=dev, device_id_type=MESH
        )

    barrier = pltpu.get_barrier_semaphore()
    peers = [(y * Z + lax.rem(z + d, Z), tp) for d in range(1, Z)]
    peers += [(lax.rem(y + d, Y) * Z + z, tp) for d in range(1, Y)]
    peers += [(ctx, right), (ctx, left)] if X > 2 else []
    peers += [(ctx, sib)]
    for peer in peers:
        pl.semaphore_signal(barrier, inc=1, device_id=peer, device_id_type=MESH)

    def quarter(k):
        return pl.ds(pl.multiple_of(k * VQ, VQ), VQ)

    load_tok = pltpu.make_async_copy(tok_h, tok, lsem.at[2])
    load_tok.start()
    load_v = pltpu.make_async_copy(vw.at[:, quarter(r)], W.at[ctx, :, pl.ds(0, VQ)], lsem.at[0])
    load_z = pltpu.make_async_copy(zw, W.at[ctx, :, pl.ds(VQ, ZH)], lsem.at[1])
    load_v.start()
    load_z.start()
    small = (
        (decay_h, decay), (phase_h, phase), (e_in_h, e_in), (e_out_h, e_out), (gain_h, gain), (bias_h, bias),
        (skip_h, skip), (rgain_h, rgain), (affine_h, affine),
    )
    loads = [pltpu.make_async_copy(a, b, lsem.at[3 + k]) for k, (a, b) in enumerate(small)]
    for c in loads:
        c.start()

    load_tok.wait()
    xb = tok[...]
    xf = xb.astype(f32)
    same = (
        lax.broadcasted_iota(jnp.int32, (CL, CL), 0) // GROUP
        == lax.broadcasted_iota(jnp.int32, (CL, CL), 1) // GROUP
    )
    same = jnp.where(same, 1.0, 0.0).astype(bf16)
    sq = xf * xf
    sq_hi = sq.astype(bf16)
    sq_lo = (sq - sq_hi.astype(f32)).astype(bf16)
    dot = functools.partial(jnp.dot, preferred_element_type=f32)
    row_sums = dot(xb, same)
    row_squares = dot(sq_hi, same) + dot(sq_lo, same)
    lower = jnp.where(
        lax.broadcasted_iota(jnp.int32, (L, L), 0) >= lax.broadcasted_iota(jnp.int32, (L, L), 1), 1.0, 0.0
    ).astype(f32)
    run_sums = dot(lower, row_sums, precision=highest)
    run_squares = dot(lower, row_squares, precision=highest)
    HID[0] = run_sums
    HID[1] = run_squares
    S1[z, 0:1] = run_sums[L - 1 : L]
    S1[z, 1:2] = run_squares[L - 1 : L]

    pl.semaphore_wait(barrier, len(peers))

    def row_peer(d):
        z2 = lax.rem(z + d, Z)
        return z2, (y * Z + z2, tp)

    def col_peer(d):
        y2 = lax.rem(y + d, Y)
        return y2, (y2 * Z + z, tp)

    def exchange(phase_at, n, mine, peer_of, source, dest):
        copies = []
        for d in range(1, n):
            who, dev = peer_of(d)
            c = pltpu.make_async_remote_copy(
                src_ref=source.at[who] if source is not dest else source.at[mine],
                dst_ref=dest.at[mine],
                send_sem=ssend.at[phase_at, d - 1],
                recv_sem=srecv.at[phase_at, d - 1],
                device_id=dev,
                device_id_type=MESH,
            )
            c.start()
            copies.append(c)

        def finish():
            for c in copies:
                c.wait_recv()
            for c in copies:
                c.wait_send()

        return finish

    def row_weights(d, k):
        z2 = lax.rem(z + d, Z)
        src = vw.at[:, quarter(lax.rem(z2, GS))] if k == 0 else zw
        cols = pl.ds(0, VQ) if k == 0 else pl.ds(VQ, ZH)
        return remote(src, W.at[ctx, :, cols], zsend.at[d - 1, k], zrecv.at[d - 1, k], (y * Z + z2, tp))

    def await_row(d, k):
        src = y * Z + lax.rem(z - d + Z, Z)
        cols = pl.ds(0, VQ) if k == 0 else pl.ds(VQ, ZH)
        ref = W.at[src, :, cols]
        remote(ref, ref, zsend.at[d - 1, k], zrecv.at[d - 1, k], (y * Z + lax.rem(z + d, Z), tp)).wait_recv()

    near = [d for pair in zip(range(1, Z), range(Z - 1, 0, -1)) for d in pair][: Z - 1]
    state = {"slot": 0, "waited": {(0, 0)}}

    def await_piece(oz, oy):
        key = (oz % Z, oy % Y)
        if key in state["waited"]:
            return
        state["waited"].add(key)
        if key[1] == 0:
            await_row(-oz % Z, 0)
            await_row(-oz % Z, 1)
        else:
            src = at(oy, oz)
            remote(W.at[src], W.at[src], wsend.at[0, 0], wrecv.at[src], (at(1, 0), tp)).wait_recv()

    def send_piece(k, i, start):
        oz, oy = plan[k][i]
        src = at(oy, oz)
        c = remote(W.at[src], W.at[src], wsend.at[k, i % DEPTH], wrecv.at[src], (at((1, -1)[k], 0), tp))
        if start:
            c.start()
        else:
            c.wait_send()

    slots = max(len(p) for p in plan)

    def pump(n):
        for _ in range(n):
            i = state["slot"]
            if i >= slots:
                return
            for k in range(2):
                if i < len(plan[k]):
                    await_piece(*plan[k][i])
                    if i >= DEPTH:
                        send_piece(k, i - DEPTH, False)
                    send_piece(k, i, True)
            state["slot"] = i + 1

    def drain():
        pump(slots)
        for k in range(2):
            n = len(plan[k])
            for i in range(max(n - DEPTH, 0), n):
                send_piece(k, i, False)
        for oy in range(Y):
            for oz in range(Z):
                await_piece(oz, oy)
        for d in range(1, Z):
            for k in range(2):
                row_weights(d, k).wait_send()

    stats_row = exchange(0, Z, z, row_peer, S1, S1)
    for d in near:
        for k in range(2):
            row_weights(d, k).start()
    load_v.wait()
    load_z.wait()
    pump(1)
    for c in loads:
        c.wait()

    sine, cosine = sin_cos(phase[...])
    dec = decay[...]
    qr, qi = dec * cosine, dec * sine
    QP[0], QP[1] = qr, qi
    ein = e_in[...]
    QP[2], QP[3] = ein * e_out[0], ein * e_out[1]
    pr, pi = qr, qi
    for k in range(1, 11):
        pr, pi = cmul(pr, pi, pr, pi)
        if k in (4, 5, 6):
            QP[2 * k - 4], QP[2 * k - 3] = pr, pi
        if k == 7:
            q7 = (pr, pi)
        if 2**k == STRETCH * Z:
            q10 = (pr, pi)
    for s in range(Z):
        for n, part in enumerate((*q7, *q10)):
            QX[s, n] = part[s * JS : (s + 1) * JS]
    for t in range(4):
        for j in range(NDIM):
            TB[t, j] = jnp.broadcast_to(QP[t, j : j + 1], (SUB, CL))

    stats_row()
    before, whole = jnp.zeros((2, CL), f32), jnp.zeros((2, CL), f32)
    for k in range(Z):
        part = S1[k]
        before = before + jnp.where(k < z, part, 0.0)
        whole = whole + part
    S2[y] = whole
    stats_col = exchange(1, Y, y, col_peer, S2, S2)
    pump(2)
    sub_row = lax.broadcasted_iota(jnp.int32, (SUB, LANES), 0)
    stats_col()
    for k in range(Y):
        before = before + jnp.where(k < y, S2[k], 0.0)
    counts = ((ctx * L + lax.broadcasted_iota(jnp.int32, (L, 1), 0)) + 1).astype(f32) * GROUP
    average = (before[0:1] + HID[0]) / counts
    spread = jnp.maximum((before[1:2] + HID[1]) / counts - average * average, 0.0)
    scaled = (tok[...].astype(f32) - average) * lax.rsqrt(spread + 1e-5)
    normed = (scaled * gain[...] + bias[...]).astype(bf16)
    NF[r, tp] = normed
    for t in range(tiles):
        N32[t] = normed[:, t * LANES : (t + 1) * LANES].astype(f32)

    def group_peer(d):
        return (y * Z + group * GS + lax.rem(r + d, GS), tp)

    group_send = [remote(NF.at[r, tp], NF.at[r, tp], gsend.at[d - 1], grecv.at[d - 1], group_peer(d)) for d in range(1, GS)]
    for c in group_send:
        c.start()

    def await_group(d):
        b = lax.rem(r - d + GS, GS)
        remote(NF.at[b, tp], NF.at[b, tp], gsend.at[d - 1], grecv.at[d - 1], group_peer(d)).wait_recv()

    def share(item, plus, ref):
        def hop(block, dev, k):
            return remote(ref(block), ref(block), xsend.at[item, k], xrecv.at[item, k], (ctx, dev))

        sent = []

        def start(c):
            c.start()
            sent.append(c)

        def send():
            if X > 2:
                start(hop(tp, right, 0))
                start(hop(tp, left, 1))
            start(hop(tp, sib, 3))

        def relay():
            if X > 2:
                hop(left, left, 0).wait_recv()
                if plus:
                    start(hop(left, right, 2))
                start(hop(left, sib, 4))
                hop(right, right, 1).wait_recv()
                if not plus:
                    start(hop(right, left, 2))
                start(hop(right, sib, 5))

        def relay_far():
            if X > 2:
                hop(far, right, 2).wait_recv()
                start(hop(far, sib, 6))

        def finish():
            hop(sib, sib, 3).wait_recv()
            if X > 2:
                for k, block in ((4, left), (5, right), (6, far)):
                    hop(block + 1 - 2 * core, sib, k).wait_recv()
            for c in sent:
                c.wait_send()

        return send, relay, relay_far, finish

    def normed_item(i):
        b = lax.rem(r - i + GS, GS)
        return share(i, i < GS // 2, lambda block: NF.at[b, block])

    normed_items = [normed_item(i) for i in range(GS)]
    mixed_items = [share(GS + t, t < tiles // 2, lambda block, t=t: MF.at[block, t]) for t in range(tiles)]
    normed_items[0][0]()

    per = L // SUB

    def first_pass(t):
        cs = pl.ds(t * LANES, LANES)

        def step(i, st):
            v = N32[t, pl.ds(i, SUB, stride=per)]
            new = []
            for j in range(NDIM):
                sr, si = st[2 * j], st[2 * j + 1]
                a, b = TB[0, j, :, cs], TB[1, j, :, cs]
                new += [a * sr - b * si + v, a * si + b * sr]
            return tuple(new)

        zero = jnp.zeros((SUB, LANES), f32)
        st = lax.fori_loop(0, per, step, (zero,) * (2 * NDIM))
        for j in range(NDIM):
            ir, ii = st[2 * j], st[2 * j + 1]
            for n, sh in enumerate((1, 2, 4)):
                fr, fi = QP[4 + 2 * n, j : j + 1, cs], QP[5 + 2 * n, j : j + 1, cs]
                rr, ri = pltpu.roll(ir, sh, 0), pltpu.roll(ii, sh, 0)
                mr, mi = cmul(fr, fi, rr, ri)
                keep = sub_row >= sh
                ir, ii = ir + jnp.where(keep, mr, 0.0), ii + jnp.where(keep, mi, 0.0)
            TOT[j // JS, j % JS : j % JS + 1, cs] = ir[SUB - 1 : SUB]
            TOT[j // JS, JS + j % JS : JS + j % JS + 1, cs] = ii[SUB - 1 : SUB]
            LOC[j, 0, :, cs] = jnp.where(sub_row >= 1, pltpu.roll(ir, 1, 0), 0.0)
            LOC[j, 1, :, cs] = jnp.where(sub_row >= 1, pltpu.roll(ii, 1, 0), 0.0)

    def sub_powers(t):
        cs = pl.ds(t * LANES, LANES)
        for j in range(NDIM):
            wr, wi = jnp.ones((SUB, LANES), f32), jnp.zeros((SUB, LANES), f32)
            for n, bit in enumerate((1, 2, 4)):
                fr, fi = QP[4 + 2 * n, j : j + 1, cs], QP[5 + 2 * n, j : j + 1, cs]
                mr, mi = cmul(wr, wi, fr, fi)
                on = (sub_row // bit) % 2 == 1
                wr, wi = jnp.where(on, mr, wr), jnp.where(on, mi, wi)
            PW[j, 0, :, cs], PW[j, 1, :, cs] = wr, wi

    for t in range(tiles):
        first_pass(t)
        pump(1)

    RS[z] = TOT[z]
    states_row = exchange(2, Z, z, row_peer, TOT, RS)
    normed_items[0][1]()
    for t in range(tiles):
        sub_powers(t)
    pump(2)
    states_row()
    q128r, q128i, q1kr, q1ki = QX[z, 0], QX[z, 1], QX[z, 2], QX[z, 3]

    def onward(sr, si, fr, fi, part):
        nr, ni = cmul(sr, si, fr, fi)
        return nr + part[0:JS], ni + part[JS : 2 * JS]

    sr, si = jnp.zeros((JS, CL), f32), jnp.zeros((JS, CL), f32)
    for k in range(Z):
        sr, si = onward(sr, si, q128r, q128i, RS[k])
    CS[y, 0:JS], CS[y, JS : 2 * JS] = sr, si
    states_col = exchange(3, Y, y, col_peer, CS, CS)
    pump(2)
    normed_items[0][2]()
    for i in range(1, GS):
        await_group(i)
        normed_items[i][0]()
    states_col()
    sr, si = jnp.zeros((JS, CL), f32), jnp.zeros((JS, CL), f32)
    for k in range(Y):
        nr, ni = onward(sr, si, q1kr, q1ki, CS[k])
        sr, si = jnp.where(k < y, nr, sr), jnp.where(k < y, ni, si)
    for k in range(Z):
        OUTS[k, 0:JS], OUTS[k, JS : 2 * JS] = sr, si
        if k + 1 < Z:
            sr, si = onward(sr, si, q128r, q128i, RS[k])
    IS[z] = OUTS[z]
    states_back = exchange(4, Z, z, row_peer, OUTS, IS)
    pump(3)
    for i in range(1, GS):
        normed_items[i][1]()
    states_back()

    def second_pass(t):
        cs = pl.ds(t * LANES, LANES)
        init = []
        for j in range(NDIM):
            gr = IS[j // JS, j % JS : j % JS + 1, cs]
            gi = IS[j // JS, JS + j % JS : JS + j % JS + 1, cs]
            mr, mi = cmul(PW[j, 0, :, cs], PW[j, 1, :, cs], gr, gi)
            init += [LOC[j, 0, :, cs] + mr, LOC[j, 1, :, cs] + mi]
        sk = skip[:, cs]

        def step(i, st):
            v = N32[t, pl.ds(i, SUB, stride=per)]
            new, total = [], sk * v
            for j in range(NDIM):
                sr, si = st[2 * j], st[2 * j + 1]
                a, b = TB[0, j, :, cs], TB[1, j, :, cs]
                nr, ni = a * sr - b * si + v, a * si + b * sr
                total = total + (TB[2, j, :, cs] * nr - TB[3, j, :, cs] * ni)
                new += [nr, ni]
            ACC[t, pl.ds(i, SUB, stride=per)] = total
            return tuple(new)

        lax.fori_loop(0, per, step, tuple(init))

    for t in range(tiles):
        second_pass(t)
        MF[tp, t] = silu(ACC[t]).astype(bf16)
        mixed_items[t][0]()
        pump(1)
    for i in range(1, GS):
        normed_items[i][2]()
    for item in mixed_items:
        item[1]()
    pump(2)
    for item in mixed_items:
        item[2]()
    drain()
    for item in normed_items:
        item[3]()
    for c in group_send:
        c.wait_send()

    def weight_rows(t, cols):
        if KR <= CL:
            n = CL // KR
            return W[t * n : (t + 1) * n, :, cols].reshape(CL, -1)
        n = KR // CL
        return W[t // n, (t % n) * CL : (t % n + 1) * CL, cols]

    back = []
    for i in range(GS):
        b = lax.rem(r + i, GS)
        acc = jnp.zeros((L, VQ), f32)
        for t in range(T):
            acc = acc + dot(NF[b, t], weight_rows(t, slice(0, VQ)))
        if i == 0:
            VR[r] = silu(acc).astype(bf16)
        else:
            VB[i - 1] = silu(acc).astype(bf16)
            c = remote(VB.at[i - 1], VR.at[r], vsend.at[i - 1], vrecv.at[i - 1], group_peer(i))
            c.start()
            back.append(c)

    for item in mixed_items:
        item[3]()
    squares = jnp.zeros((L, LANES), f32)
    for t in range(T):
        for k in range(tiles):
            m = MF[t, k].astype(f32)
            squares = squares + m * m
    rinv = lax.rsqrt(jnp.sum(squares, axis=-1, keepdims=True) * (1.0 / (T * CL)) + 1e-6)
    z_total = jnp.zeros((L, ZH), f32)
    for t in range(T):
        m = jnp.concatenate([MF[t, k] for k in range(tiles)], axis=1).astype(f32)
        m = (m * rinv * rgain[:, t * CL : (t + 1) * CL]).astype(bf16)
        z_total = z_total + dot(m, weight_rows(t, slice(VQ, VQ + ZH)))
    queries = (z_total * affine[0:1] + affine[1:2]).astype(bf16)
    keys = (z_total * affine[2:3] + affine[3:4]).astype(bf16)
    scores = lax.dot_general(
        queries, keys, (((1,), (1,)), ((), ())), preferred_element_type=f32
    ) * (1.0 / ZH**0.5)
    causal = lax.broadcasted_iota(jnp.int32, (L, L), 0) >= lax.broadcasted_iota(jnp.int32, (L, L), 1)
    scores = jnp.where(causal, scores, -1e30)
    weights = jnp.exp(scores - jnp.max(scores, axis=-1, keepdims=True))
    probabilities = (weights / jnp.sum(weights, axis=-1, keepdims=True)).astype(bf16)

    for c in back:
        c.wait()
    for k in range(GS):
        out[:, k * VQ : (k + 1) * VQ] = dot(probabilities, VR[k]).astype(bf16)


def grid_of(mesh):
    n = mesh.shape["ctx"]
    rows = 1
    while rows * rows < n:
        rows *= 2
    return rows, n // rows


def solution(mesh):
    Y, Z = grid_of(mesh)
    T = mesh.shape["tp"]
    X = T // 2
    plan = ring_lists(Y, Z)
    GS = min(4, Z)

    def body(tok, gain, bias, decay, phase, e_in, e_out, skip, rgain, zw, vw, affine):
        L, CL = tok.shape
        KR, VC = vw.shape
        JS = NDIM // Z
        row = lambda a: a.reshape(1, -1)
        vm = pl.BlockSpec(memory_space=pltpu.VMEM)
        hbm = pl.BlockSpec(memory_space=pl.ANY)
        V = pltpu.VMEM
        dma = pltpu.SemaphoreType.DMA
        most = max(Y, Z) - 1
        return pl.pallas_call(
            functools.partial(kernel, Y, Z, X, GS, plan),
            out_shape=jax.ShapeDtypeStruct((L, VC), bf16),
            in_specs=[hbm] * 12,
            out_specs=vm,
            scratch_shapes=[
                V((L, CL), bf16),
                V((1, CL), f32),
                V((1, CL), f32),
                *[V((NDIM, CL), f32)] * 3,
                V((2, NDIM, CL), f32),
                V((1, CL), f32),
                V((1, T * CL), f32),
                V((4, ZH), f32),
                V((Y * Z, KR, VC // GS + ZH), bf16),
                V((GS, T, L, CL), bf16),
                V((T, CL // LANES, L, LANES), bf16),
                V((GS - 1, L, VC // GS), bf16),
                V((GS, L, VC // GS), bf16),
                V((CL // LANES, L, LANES), f32),
                V((4, NDIM, SUB, CL), f32),
                V((NDIM, 2, SUB, CL), f32),
                V((NDIM, 2, SUB, CL), f32),
                V((10, NDIM, CL), f32),
                V((Z, 4, JS, CL), f32),
                V((Z, 2 * JS, CL), f32),
                V((Z, 2 * JS, CL), f32),
                V((Y, 2 * JS, CL), f32),
                V((Z, 2 * JS, CL), f32),
                V((Z, 2 * JS, CL), f32),
                V((Z, 2, CL), f32),
                V((Y, 2, CL), f32),
                V((CL // LANES, L, LANES), f32),
                V((2, L, CL), f32),
                dma((2, DEPTH)),
                dma((Y * Z,)),
                dma((Z - 1, 2)),
                dma((Z - 1, 2)),
                dma((12,)),
                dma((5, most)),
                dma((5, most)),
                dma((GS + CL // LANES, 7)),
                dma((GS + CL // LANES, 7)),
                dma((GS - 1,)),
                dma((GS - 1,)),
                dma((GS - 1,)),
                dma((GS - 1,)),
            ],
            compiler_params=pltpu.CompilerParams(
                collective_id=0, has_side_effects=True, vmem_limit_bytes=60 << 20
            ),
        )(tok, row(gain), row(bias), decay, phase, e_in, e_out, row(skip), row(rgain), zw, vw, affine)

    in_specs = (
        P("ctx", "tp"), P("tp"), P("tp"), P(None, "tp"), P(None, "tp"), P(None, "tp"), P(None, None, "tp"),
        P("tp"), P(), P("ctx", "tp"), P("ctx", "tp"), P(None, "tp"),
    )
    return jax.shard_map(body, mesh=mesh, in_specs=in_specs, out_specs=P("ctx", "tp"), check_vma=False)
```

```python
import functools
import math

import jax
import jax.numpy as jnp
from jax import lax
from jax.experimental import pallas as pl
from jax.experimental.pallas import tpu as pltpu
from jax.sharding import PartitionSpec as P

NDIM = 16
ZH = 128
GROUP = 64
STRETCH = 128
SUB = 8
LANES = 128
DEPTH = 2
MESH = pl.DeviceIdType.MESH
f32 = jnp.float32
bf16 = jnp.bfloat16
highest = lax.Precision.HIGHEST


def ring_lists(Y, Z):
    columns = [0]
    for d in range(1, Z // 2 + 1):
        columns += [-d] if 2 * d == Z else [-d, d]
    plus, minus = [], []
    for e in range(Y // 2 + 1):
        for i, oz in enumerate(columns):
            more, less = Y // 2, (Y - 1) // 2
            if e < (less if i % 2 else more):
                plus.append((oz, -e))
            if e < (more if i % 2 else less):
                minus.append((oz, e))
    return plus, minus


def silu(v):
    return v * (1.0 / (1.0 + jnp.exp(-v)))


def cmul(ar, ai, br, bi):
    return ar * br - ai * bi, ar * bi + ai * br


def sin_cos(p):
    s = p * p
    sine = p * (1.0 + s * (-1 / 6 + s * (1 / 120 + s * (-1 / 5040 + s * (1 / 362880 - s / 39916800)))))
    cosine = 1.0 + s * (
        -0.5 + s * (1 / 24 + s * (-1 / 720 + s * (1 / 40320 + s * (-1 / 3628800 + s / 479001600))))
    )
    return sine, cosine


def kernel(
    Y, Z, X, GS, plan,
    tok_h, gain_h, bias_h, decay_h, phase_h, e_in_h, e_out_h, skip_h, rgain_h, zw, vw, affine_h,
    out,
    tok, gain, bias, decay, phase, e_in, e_out, skip, rgain, affine,
    W, NF, MF, NRM, VACC, VB, VR, N32, TB, LOC, PW, QP, QX, TOT, RS, CS, OUTS, IS, S1, S2, ACC, HID,
    wsend, wrecv, zsend, zrecv, lsem, ssend, srecv, xsend, xrecv, gsend, grecv, vsend, vrecv,
):
    ctx, tp = lax.axis_index("ctx"), lax.axis_index("tp")
    y, z = ctx // Z, ctx % Z
    x, core = tp // 2, tp % 2
    group, r = z // GS, z % GS
    _, T, L, CL = NF.shape
    KR = W.shape[1]
    VC = vw.shape[1]
    VQ = VC // GS
    JS = NDIM // Z
    tiles = CL // LANES
    sib = x * 2 + (1 - core)
    right, left, far = (lax.rem(x + d, X) * 2 + core for d in (1, X - 1, X // 2))

    def at(dy, dz):
        return lax.rem(y + dy + Y, Y) * Z + lax.rem(z + dz + Z, Z)

    def remote(src, dst, send, recv, dev):
        return pltpu.make_async_remote_copy(
            src_ref=src, dst_ref=dst, send_sem=send, recv_sem=recv, device_id=dev, device_id_type=MESH
        )

    barrier = pltpu.get_barrier_semaphore()
    peers = [(y * Z + lax.rem(z + d, Z), tp) for d in range(1, Z)]
    peers += [(lax.rem(y + d, Y) * Z + z, tp) for d in range(1, Y)]
    peers += [(ctx, right), (ctx, left)] if X > 2 else []
    peers += [(ctx, sib)]
    for peer in peers:
        pl.semaphore_signal(barrier, inc=1, device_id=peer, device_id_type=MESH)

    def quarter(k):
        return pl.ds(pl.multiple_of(k * VQ, VQ), VQ)

    load_tok = pltpu.make_async_copy(tok_h, tok, lsem.at[2])
    load_tok.start()
    load_v = pltpu.make_async_copy(vw.at[:, quarter(r)], W.at[ctx, :, pl.ds(0, VQ)], lsem.at[0])
    load_z = pltpu.make_async_copy(zw, W.at[ctx, :, pl.ds(VQ, ZH)], lsem.at[1])
    load_v.start()
    load_z.start()
    small = (
        (decay_h, decay), (phase_h, phase), (e_in_h, e_in), (e_out_h, e_out), (gain_h, gain), (bias_h, bias),
        (skip_h, skip), (rgain_h, rgain), (affine_h, affine),
    )
    loads = [pltpu.make_async_copy(a, b, lsem.at[3 + k]) for k, (a, b) in enumerate(small)]
    for c in loads:
        c.start()

    load_tok.wait()
    xb = tok[...]
    xf = xb.astype(f32)
    same = (
        lax.broadcasted_iota(jnp.int32, (CL, CL), 0) // GROUP
        == lax.broadcasted_iota(jnp.int32, (CL, CL), 1) // GROUP
    )
    same = jnp.where(same, 1.0, 0.0).astype(bf16)
    sq = xf * xf
    sq_hi = sq.astype(bf16)
    sq_lo = (sq - sq_hi.astype(f32)).astype(bf16)
    dot = functools.partial(jnp.dot, preferred_element_type=f32)
    row_sums = dot(xb, same)
    row_squares = dot(sq_hi, same) + dot(sq_lo, same)
    lower = jnp.where(
        lax.broadcasted_iota(jnp.int32, (L, L), 0) >= lax.broadcasted_iota(jnp.int32, (L, L), 1), 1.0, 0.0
    ).astype(f32)
    run_sums = dot(lower, row_sums, precision=highest)
    run_squares = dot(lower, row_squares, precision=highest)
    HID[0] = run_sums
    HID[1] = run_squares
    S1[z, 0:1] = run_sums[L - 1 : L]
    S1[z, 1:2] = run_squares[L - 1 : L]

    pl.semaphore_wait(barrier, len(peers))

    def row_peer(d):
        z2 = lax.rem(z + d, Z)
        return z2, (y * Z + z2, tp)

    def col_peer(d):
        y2 = lax.rem(y + d, Y)
        return y2, (y2 * Z + z, tp)

    def exchange(phase_at, n, mine, peer_of, source, dest):
        copies = []
        for d in range(1, n):
            who, dev = peer_of(d)
            c = pltpu.make_async_remote_copy(
                src_ref=source.at[who] if source is not dest else source.at[mine],
                dst_ref=dest.at[mine],
                send_sem=ssend.at[phase_at, d - 1],
                recv_sem=srecv.at[phase_at, d - 1],
                device_id=dev,
                device_id_type=MESH,
            )
            c.start()
            copies.append(c)

        def finish():
            for c in copies:
                c.wait_recv()
            for c in copies:
                c.wait_send()

        return finish

    def row_weights(d, k):
        z2 = lax.rem(z + d, Z)
        src = vw.at[:, quarter(lax.rem(z2, GS))] if k == 0 else zw
        cols = pl.ds(0, VQ) if k == 0 else pl.ds(VQ, ZH)
        return remote(src, W.at[ctx, :, cols], zsend.at[d - 1, k], zrecv.at[d - 1, k], (y * Z + z2, tp))

    def await_row(d, k):
        src = y * Z + lax.rem(z - d + Z, Z)
        cols = pl.ds(0, VQ) if k == 0 else pl.ds(VQ, ZH)
        ref = W.at[src, :, cols]
        remote(ref, ref, zsend.at[d - 1, k], zrecv.at[d - 1, k], (y * Z + lax.rem(z + d, Z), tp)).wait_recv()

    near = [d for pair in zip(range(1, Z), range(Z - 1, 0, -1)) for d in pair][: Z - 1]
    state = {"slot": 0, "waited": {(0, 0)}}

    def await_piece(oz, oy):
        key = (oz % Z, oy % Y)
        if key in state["waited"]:
            return
        state["waited"].add(key)
        if key[1] == 0:
            await_row(-oz % Z, 0)
            await_row(-oz % Z, 1)
        else:
            src = at(oy, oz)
            remote(W.at[src], W.at[src], wsend.at[0, 0], wrecv.at[src], (at(1, 0), tp)).wait_recv()

    def send_piece(k, i, start):
        oz, oy = plan[k][i]
        src = at(oy, oz)
        c = remote(W.at[src], W.at[src], wsend.at[k, i % DEPTH], wrecv.at[src], (at((1, -1)[k], 0), tp))
        if start:
            c.start()
        else:
            c.wait_send()

    slots = max(len(p) for p in plan)

    def pump(n):
        for _ in range(n):
            i = state["slot"]
            if i >= slots:
                return
            for k in range(2):
                if i < len(plan[k]):
                    await_piece(*plan[k][i])
                    if i >= DEPTH:
                        send_piece(k, i - DEPTH, False)
                    send_piece(k, i, True)
            state["slot"] = i + 1

    def drain():
        pump(slots)
        for k in range(2):
            n = len(plan[k])
            for i in range(max(n - DEPTH, 0), n):
                send_piece(k, i, False)
        for oy in range(Y):
            for oz in range(Z):
                await_piece(oz, oy)
        for d in range(1, Z):
            for k in range(2):
                row_weights(d, k).wait_send()

    stats_row = exchange(0, Z, z, row_peer, S1, S1)
    for d in near:
        for k in range(2):
            row_weights(d, k).start()
    load_v.wait()
    load_z.wait()
    pump(1)
    for c in loads:
        c.wait()

    sine, cosine = sin_cos(phase[...])
    dec = decay[...]
    qr, qi = dec * cosine, dec * sine
    QP[0], QP[1] = qr, qi
    ein = e_in[...]
    QP[2], QP[3] = ein * e_out[0], ein * e_out[1]
    pr, pi = qr, qi
    for k in range(1, 11):
        pr, pi = cmul(pr, pi, pr, pi)
        if k in (4, 5, 6):
            QP[2 * k - 4], QP[2 * k - 3] = pr, pi
        if k == 7:
            q7 = (pr, pi)
        if 2**k == STRETCH * Z:
            q10 = (pr, pi)
    for s in range(Z):
        for n, part in enumerate((*q7, *q10)):
            QX[s, n] = part[s * JS : (s + 1) * JS]
    for t in range(4):
        for j in range(NDIM):
            TB[t, j] = jnp.broadcast_to(QP[t, j : j + 1], (SUB, CL))

    pump(2)
    stats_row()
    before, whole = jnp.zeros((2, CL), f32), jnp.zeros((2, CL), f32)
    for k in range(Z):
        part = S1[k]
        before = before + jnp.where(k < z, part, 0.0)
        whole = whole + part
    S2[y] = whole
    stats_col = exchange(1, Y, y, col_peer, S2, S2)
    pump(4)
    sub_row = lax.broadcasted_iota(jnp.int32, (SUB, LANES), 0)
    stats_col()
    for k in range(Y):
        before = before + jnp.where(k < y, S2[k], 0.0)
    counts = ((ctx * L + lax.broadcasted_iota(jnp.int32, (L, 1), 0)) + 1).astype(f32) * GROUP
    average = (before[0:1] + HID[0]) / counts
    spread = jnp.maximum((before[1:2] + HID[1]) / counts - average * average, 0.0)
    scaled = (tok[...].astype(f32) - average) * lax.rsqrt(spread + 1e-5)
    normed = (scaled * gain[...] + bias[...]).astype(bf16)
    NF[r, tp] = normed
    for t in range(tiles):
        N32[t] = normed[:, t * LANES : (t + 1) * LANES].astype(f32)

    def partner(d):
        low, high = r % 2, r // 2
        return (low + d) % 2 + 2 * ((high + d // 2) % 2)

    def group_peer(d):
        return (y * Z + group * GS + partner(d), tp)

    def group_copy(d, b):
        return remote(NF.at[b, tp], NF.at[b, tp], gsend.at[d - 1], grecv.at[d - 1], group_peer(d))

    def await_group(d):
        group_copy(d, partner(d)).wait_recv()

    group_copy(1, r).start()

    def share(item, plus, ref):
        def hop(block, dev, k):
            return remote(ref(block), ref(block), xsend.at[item, k], xrecv.at[item, k], (ctx, dev))

        sent = []

        def start(c):
            c.start()
            sent.append(c)

        def send():
            if X > 2:
                start(hop(tp, right, 0))
                start(hop(tp, left, 1))
            start(hop(tp, sib, 3))

        def relay():
            if X > 2:
                hop(left, left, 0).wait_recv()
                if plus:
                    start(hop(left, right, 2))
                start(hop(left, sib, 4))
                hop(right, right, 1).wait_recv()
                if not plus:
                    start(hop(right, left, 2))
                start(hop(right, sib, 5))

        def relay_far():
            if X > 2:
                hop(far, right, 2).wait_recv()
                start(hop(far, sib, 6))

        def finish():
            hop(sib, sib, 3).wait_recv()
            if X > 2:
                for k, block in ((4, left), (5, right), (6, far)):
                    hop(block + 1 - 2 * core, sib, k).wait_recv()
            for c in sent:
                c.wait_send()

        return send, relay, relay_far, finish

    def normed_item(i):
        b = partner(i)
        return share(i, i < GS // 2, lambda block: NF.at[b, block])

    normed_items = [normed_item(i) for i in range(GS)]
    mixed_items = [share(GS + t, t < tiles // 2, lambda block, t=t: MF.at[block, t]) for t in range(tiles)]
    normed_items[0][0]()

    per = L // SUB

    def first_pass(t):
        cs = pl.ds(t * LANES, LANES)

        def step(i, st):
            v = N32[t, pl.ds(i, SUB, stride=per)]
            new = []
            for j in range(NDIM):
                sr, si = st[2 * j], st[2 * j + 1]
                a, b = TB[0, j, :, cs], TB[1, j, :, cs]
                new += [a * sr - b * si + v, a * si + b * sr]
            return tuple(new)

        zero = jnp.zeros((SUB, LANES), f32)
        st = lax.fori_loop(0, per, step, (zero,) * (2 * NDIM))
        for j in range(NDIM):
            ir, ii = st[2 * j], st[2 * j + 1]
            for n, sh in enumerate((1, 2, 4)):
                fr, fi = QP[4 + 2 * n, j : j + 1, cs], QP[5 + 2 * n, j : j + 1, cs]
                rr, ri = pltpu.roll(ir, sh, 0), pltpu.roll(ii, sh, 0)
                mr, mi = cmul(fr, fi, rr, ri)
                keep = sub_row >= sh
                ir, ii = ir + jnp.where(keep, mr, 0.0), ii + jnp.where(keep, mi, 0.0)
            TOT[j // JS, j % JS : j % JS + 1, cs] = ir[SUB - 1 : SUB]
            TOT[j // JS, JS + j % JS : JS + j % JS + 1, cs] = ii[SUB - 1 : SUB]
            LOC[j, 0, :, cs] = jnp.where(sub_row >= 1, pltpu.roll(ir, 1, 0), 0.0)
            LOC[j, 1, :, cs] = jnp.where(sub_row >= 1, pltpu.roll(ii, 1, 0), 0.0)

    def sub_powers(t):
        cs = pl.ds(t * LANES, LANES)
        for j in range(NDIM):
            wr, wi = jnp.ones((SUB, LANES), f32), jnp.zeros((SUB, LANES), f32)
            for n, bit in enumerate((1, 2, 4)):
                fr, fi = QP[4 + 2 * n, j : j + 1, cs], QP[5 + 2 * n, j : j + 1, cs]
                mr, mi = cmul(wr, wi, fr, fi)
                on = (sub_row // bit) % 2 == 1
                wr, wi = jnp.where(on, mr, wr), jnp.where(on, mi, wi)
            PW[j, 0, :, cs], PW[j, 1, :, cs] = wr, wi

    for t in range(tiles):
        first_pass(t)
        if t % 2:
            pump(1)

    RS[z] = TOT[z]
    states_row = exchange(2, Z, z, row_peer, TOT, RS)
    normed_items[0][1]()
    for t in range(tiles):
        sub_powers(t)
    pump(2)
    await_group(1)
    normed_items[1][0]()
    pump(2)
    states_row()
    q128r, q128i, q1kr, q1ki = QX[z, 0], QX[z, 1], QX[z, 2], QX[z, 3]

    def onward(sr, si, fr, fi, part):
        nr, ni = cmul(sr, si, fr, fi)
        return nr + part[0:JS], ni + part[JS : 2 * JS]

    sr, si = jnp.zeros((JS, CL), f32), jnp.zeros((JS, CL), f32)
    for k in range(Z):
        sr, si = onward(sr, si, q128r, q128i, RS[k])
    CS[y, 0:JS], CS[y, JS : 2 * JS] = sr, si
    states_col = exchange(3, Y, y, col_peer, CS, CS)
    for d in range(2, min(3, GS)):
        group_copy(d, r).start()
    pump(2)
    normed_items[0][2]()
    normed_items[1][1]()
    pump(2)
    states_col()
    sr, si = jnp.zeros((JS, CL), f32), jnp.zeros((JS, CL), f32)
    for k in range(Y):
        nr, ni = onward(sr, si, q1kr, q1ki, CS[k])
        sr, si = jnp.where(k < y, nr, sr), jnp.where(k < y, ni, si)
    for k in range(Z):
        OUTS[k, 0:JS], OUTS[k, JS : 2 * JS] = sr, si
        if k + 1 < Z:
            sr, si = onward(sr, si, q128r, q128i, RS[k])
    IS[z] = OUTS[z]
    states_back = exchange(4, Z, z, row_peer, OUTS, IS)
    pump(2)
    normed_items[1][2]()
    for d in range(2, min(3, GS)):
        await_group(d)
        normed_items[d][0]()
    pump(2)
    states_back()
    for d in range(3, GS):
        group_copy(d, r).start()

    def second_pass(t):
        cs = pl.ds(t * LANES, LANES)
        init = []
        for j in range(NDIM):
            gr = IS[j // JS, j % JS : j % JS + 1, cs]
            gi = IS[j // JS, JS + j % JS : JS + j % JS + 1, cs]
            mr, mi = cmul(PW[j, 0, :, cs], PW[j, 1, :, cs], gr, gi)
            init += [LOC[j, 0, :, cs] + mr, LOC[j, 1, :, cs] + mi]
        sk = skip[:, cs]

        def step(i, st):
            v = N32[t, pl.ds(i, SUB, stride=per)]
            new, total = [], sk * v
            for j in range(NDIM):
                sr, si = st[2 * j], st[2 * j + 1]
                a, b = TB[0, j, :, cs], TB[1, j, :, cs]
                nr, ni = a * sr - b * si + v, a * si + b * sr
                total = total + (TB[2, j, :, cs] * nr - TB[3, j, :, cs] * ni)
                new += [nr, ni]
            ACC[t, pl.ds(i, SUB, stride=per)] = total
            return tuple(new)

        lax.fori_loop(0, per, step, tuple(init))

    for t in range(tiles):
        second_pass(t)
        MF[tp, t] = silu(ACC[t]).astype(bf16)
        mixed_items[t][0]()
        if t % 2:
            pump(1)
    pump(1)
    for d in range(2, min(3, GS)):
        normed_items[d][1]()
    for item in mixed_items:
        item[1]()
    for d in range(3, GS):
        await_group(d)
        normed_items[d][0]()
    pump(2)
    for item in mixed_items:
        item[2]()
    for d in range(2, min(3, GS)):
        normed_items[d][2]()
    pump(2)
    for d in range(3, GS):
        normed_items[d][1]()
    for item in mixed_items:
        item[3]()

    squares = jnp.zeros((L, LANES), f32)
    for t in range(T):
        for k in range(tiles):
            m = MF[t, k].astype(f32)
            squares = squares + m * m
    rinv = lax.rsqrt(jnp.sum(squares, axis=-1, keepdims=True) * (1.0 / (T * CL)) + 1e-6)
    for t in range(T):
        m = jnp.concatenate([MF[t, k] for k in range(tiles)], axis=1).astype(f32)
        NRM[t] = (m * rinv * rgain[:, t * CL : (t + 1) * CL]).astype(bf16)
    pump(2)
    for d in range(3, GS):
        normed_items[d][2]()
    for item in normed_items:
        item[3]()
    for d in range(1, GS):
        group_copy(d, r).wait_send()

    def weight_rows(t, cols):
        if KR <= CL:
            n = CL // KR
            return W[t * n : (t + 1) * n, :, cols].reshape(CL, -1)
        n = KR // CL
        return W[t // n, (t % n) * CL : (t % n + 1) * CL, cols]

    by_row = T == Y
    if by_row:
        order = [0] + [o for e in range(1, Y // 2 + 1) for o in ((-e, e) if 2 * e < Y else (-e,))]
        for n, oy in enumerate(order):
            if n == len(order) // 2 + 1:
                drain()
            for oz in range(Z):
                await_piece(oz, oy)
            t = lax.rem(y + oy + Y, Y)
            w = W[pl.ds(pl.multiple_of(t * Z, Z), Z), :, 0:VQ].reshape(CL, VQ)
            part = dot(NF[:, t].reshape(GS * L, CL), w)
            VACC[...] = part if n == 0 else VACC[...] + part
    else:
        drain()
        for t in range(T):
            part = dot(NF[:, t].reshape(GS * L, CL), weight_rows(t, slice(0, VQ)))
            VACC[...] = part if t == 0 else VACC[...] + part
    back = []
    for i in (*range(1, GS), 0):
        rows = pl.ds(pl.multiple_of(partner(i) * L, L), L)
        if i == 0:
            VR[r] = silu(VACC[rows]).astype(bf16)
        else:
            VB[i - 1] = silu(VACC[rows]).astype(bf16)
            c = remote(VB.at[i - 1], VR.at[r], vsend.at[i - 1], vrecv.at[i - 1], group_peer(i))
            c.start()
            back.append(c)

    z_total = jnp.zeros((L, ZH), f32)
    for t in range(T):
        z_total = z_total + dot(NRM[t], weight_rows(t, slice(VQ, VQ + ZH)))
    queries = (z_total * affine[0:1] + affine[1:2]).astype(bf16)
    keys = (z_total * affine[2:3] + affine[3:4]).astype(bf16)
    scores = lax.dot_general(
        queries, keys, (((1,), (1,)), ((), ())), preferred_element_type=f32
    ) * (1.0 / ZH**0.5)
    causal = lax.broadcasted_iota(jnp.int32, (L, L), 0) >= lax.broadcasted_iota(jnp.int32, (L, L), 1)
    scores = jnp.where(causal, scores, -1e30)
    weights = jnp.exp(scores - jnp.max(scores, axis=-1, keepdims=True))
    probabilities = (weights / jnp.sum(weights, axis=-1, keepdims=True)).astype(bf16)

    for c in back:
        c.wait()
    for k in range(GS):
        out[:, k * VQ : (k + 1) * VQ] = dot(probabilities, VR[k]).astype(bf16)


def grid_of(mesh):
    n = mesh.shape["ctx"]
    rows = 1
    while rows * rows < n:
        rows *= 2
    return rows, n // rows


def solution(mesh):
    Y, Z = grid_of(mesh)
    T = mesh.shape["tp"]
    X = T // 2
    plan = ring_lists(Y, Z)
    GS = min(4, Z)

    def body(tok, gain, bias, decay, phase, e_in, e_out, skip, rgain, zw, vw, affine):
        L, CL = tok.shape
        KR, VC = vw.shape
        JS = NDIM // Z
        row = lambda a: a.reshape(1, -1)
        vm = pl.BlockSpec(memory_space=pltpu.VMEM)
        hbm = pl.BlockSpec(memory_space=pl.ANY)
        V = pltpu.VMEM
        dma = pltpu.SemaphoreType.DMA
        most = max(Y, Z) - 1
        return pl.pallas_call(
            functools.partial(kernel, Y, Z, X, GS, plan),
            out_shape=jax.ShapeDtypeStruct((L, VC), bf16),
            in_specs=[hbm] * 12,
            out_specs=vm,
            scratch_shapes=[
                V((L, CL), bf16),
                V((1, CL), f32),
                V((1, CL), f32),
                *[V((NDIM, CL), f32)] * 3,
                V((2, NDIM, CL), f32),
                V((1, CL), f32),
                V((1, T * CL), f32),
                V((4, ZH), f32),
                V((Y * Z, KR, VC // GS + ZH), bf16),
                V((GS, T, L, CL), bf16),
                V((T, CL // LANES, L, LANES), bf16),
                V((T, L, CL), bf16),
                V((GS * L, VC // GS), f32),
                V((GS - 1, L, VC // GS), bf16),
                V((GS, L, VC // GS), bf16),
                V((CL // LANES, L, LANES), f32),
                V((4, NDIM, SUB, CL), f32),
                V((NDIM, 2, SUB, CL), f32),
                V((NDIM, 2, SUB, CL), f32),
                V((10, NDIM, CL), f32),
                V((Z, 4, JS, CL), f32),
                V((Z, 2 * JS, CL), f32),
                V((Z, 2 * JS, CL), f32),
                V((Y, 2 * JS, CL), f32),
                V((Z, 2 * JS, CL), f32),
                V((Z, 2 * JS, CL), f32),
                V((Z, 2, CL), f32),
                V((Y, 2, CL), f32),
                V((CL // LANES, L, LANES), f32),
                V((2, L, CL), f32),
                dma((2, DEPTH)),
                dma((Y * Z,)),
                dma((Z - 1, 2)),
                dma((Z - 1, 2)),
                dma((12,)),
                dma((5, most)),
                dma((5, most)),
                dma((GS + CL // LANES, 7)),
                dma((GS + CL // LANES, 7)),
                dma((GS - 1,)),
                dma((GS - 1,)),
                dma((GS - 1,)),
                dma((GS - 1,)),
            ],
            compiler_params=pltpu.CompilerParams(
                collective_id=0, has_side_effects=True, vmem_limit_bytes=60 << 20
            ),
        )(tok, row(gain), row(bias), decay, phase, e_in, e_out, row(skip), row(rgain), zw, vw, affine)

    in_specs = (
        P("ctx", "tp"), P("tp"), P("tp"), P(None, "tp"), P(None, "tp"), P(None, "tp"), P(None, None, "tp"),
        P("tp"), P(), P("ctx", "tp"), P("ctx", "tp"), P(None, "tp"),
    )
    return jax.shard_map(body, mesh=mesh, in_specs=in_specs, out_specs=P("ctx", "tp"), check_vma=False)
```

```python
import functools
import math

import jax
import jax.numpy as jnp
from jax import lax
from jax.experimental import pallas as pl
from jax.experimental.pallas import tpu as pltpu
from jax.sharding import PartitionSpec as P

NDIM = 16
ZH = 128
GROUP = 64
STRETCH = 128
SUB = 8
LANES = 128
DEPTH = 2
MESH = pl.DeviceIdType.MESH
f32 = jnp.float32
bf16 = jnp.bfloat16
highest = lax.Precision.HIGHEST


def ring_lists(Y, Z):
    columns = [0]
    for d in range(1, Z // 2 + 1):
        columns += [-d] if 2 * d == Z else [-d, d]
    plus, minus = [], []
    for e in range(Y // 2 + 1):
        for i, oz in enumerate(columns):
            more, less = Y // 2, (Y - 1) // 2
            if e < (less if i % 2 else more):
                plus.append((oz, -e))
            if e < (more if i % 2 else less):
                minus.append((oz, e))
    return plus, minus


def silu(v):
    return v * (1.0 / (1.0 + jnp.exp(-v)))


def cmul(ar, ai, br, bi):
    return ar * br - ai * bi, ar * bi + ai * br


def sin_cos(p):
    s = p * p
    sine = p * (1.0 + s * (-1 / 6 + s * (1 / 120 + s * (-1 / 5040 + s * (1 / 362880 - s / 39916800)))))
    cosine = 1.0 + s * (
        -0.5 + s * (1 / 24 + s * (-1 / 720 + s * (1 / 40320 + s * (-1 / 3628800 + s / 479001600))))
    )
    return sine, cosine


def kernel(
    Y, Z, X, GS, plan,
    tok_h, gain_h, bias_h, decay_h, phase_h, e_in_h, e_out_h, skip_h, rgain_h, zw, vw, affine_h,
    out,
    tok, gain, bias, decay, phase, e_in, e_out, skip, rgain, affine,
    W, NF, MF, NRM, VACC, VB, VR, N32, TB, LOC, PW, QP, QX, TOT, RS, CS, OUTS, IS, S1, S2, ACC, HID,
    wsend, wrecv, zsend, zrecv, lsem, ssend, srecv, xsend, xrecv, gsend, grecv, vsend, vrecv,
):
    ctx, tp = lax.axis_index("ctx"), lax.axis_index("tp")
    y, z = ctx // Z, ctx % Z
    x, core = tp // 2, tp % 2
    group, r = z // GS, z % GS
    _, T, L, CL = NF.shape
    KR = W.shape[1]
    VC = vw.shape[1]
    VQ = VC // GS
    JS = NDIM // Z
    tiles = CL // LANES
    sib = x * 2 + (1 - core)
    right, left, far = (lax.rem(x + d, X) * 2 + core for d in (1, X - 1, X // 2))

    def at(dy, dz):
        return lax.rem(y + dy + Y, Y) * Z + lax.rem(z + dz + Z, Z)

    def remote(src, dst, send, recv, dev):
        return pltpu.make_async_remote_copy(
            src_ref=src, dst_ref=dst, send_sem=send, recv_sem=recv, device_id=dev, device_id_type=MESH
        )

    barrier = pltpu.get_barrier_semaphore()
    peers = [(y * Z + lax.rem(z + d, Z), tp) for d in range(1, Z)]
    peers += [(lax.rem(y + d, Y) * Z + z, tp) for d in range(1, Y)]
    peers += [(ctx, right), (ctx, left)] if X > 2 else []
    peers += [(ctx, sib)]
    for peer in peers:
        pl.semaphore_signal(barrier, inc=1, device_id=peer, device_id_type=MESH)

    def quarter(k):
        return pl.ds(pl.multiple_of(k * VQ, VQ), VQ)

    load_tok = pltpu.make_async_copy(tok_h, tok, lsem.at[2])
    load_tok.start()
    load_v = pltpu.make_async_copy(vw.at[:, quarter(r)], W.at[ctx, :, pl.ds(0, VQ)], lsem.at[0])
    load_z = pltpu.make_async_copy(zw, W.at[ctx, :, pl.ds(VQ, ZH)], lsem.at[1])
    load_v.start()
    load_z.start()
    small = (
        (decay_h, decay), (phase_h, phase), (e_in_h, e_in), (e_out_h, e_out), (gain_h, gain), (bias_h, bias),
        (skip_h, skip), (rgain_h, rgain), (affine_h, affine),
    )
    loads = [pltpu.make_async_copy(a, b, lsem.at[3 + k]) for k, (a, b) in enumerate(small)]
    for c in loads:
        c.start()

    load_tok.wait()
    xb = tok[...]
    xf = xb.astype(f32)
    same = (
        lax.broadcasted_iota(jnp.int32, (CL, CL), 0) // GROUP
        == lax.broadcasted_iota(jnp.int32, (CL, CL), 1) // GROUP
    )
    same = jnp.where(same, 1.0, 0.0).astype(bf16)
    sq = xf * xf
    sq_hi = sq.astype(bf16)
    sq_lo = (sq - sq_hi.astype(f32)).astype(bf16)
    dot = functools.partial(jnp.dot, preferred_element_type=f32)
    row_sums = dot(xb, same)
    row_squares = dot(sq_hi, same) + dot(sq_lo, same)
    lower = jnp.where(
        lax.broadcasted_iota(jnp.int32, (L, L), 0) >= lax.broadcasted_iota(jnp.int32, (L, L), 1), 1.0, 0.0
    ).astype(f32)
    run_sums = dot(lower, row_sums, precision=highest)
    run_squares = dot(lower, row_squares, precision=highest)
    HID[0] = run_sums
    HID[1] = run_squares
    S1[z, 0:1] = run_sums[L - 1 : L]
    S1[z, 1:2] = run_squares[L - 1 : L]

    pl.semaphore_wait(barrier, len(peers))

    def row_peer(d):
        z2 = lax.rem(z + d, Z)
        return z2, (y * Z + z2, tp)

    def col_peer(d):
        y2 = lax.rem(y + d, Y)
        return y2, (y2 * Z + z, tp)

    def exchange(phase_at, n, mine, peer_of, source, dest):
        copies = []
        for d in range(1, n):
            who, dev = peer_of(d)
            c = pltpu.make_async_remote_copy(
                src_ref=source.at[who] if source is not dest else source.at[mine],
                dst_ref=dest.at[mine],
                send_sem=ssend.at[phase_at, d - 1],
                recv_sem=srecv.at[phase_at, d - 1],
                device_id=dev,
                device_id_type=MESH,
            )
            c.start()
            copies.append(c)

        def finish():
            for c in copies:
                c.wait_recv()
            for c in copies:
                c.wait_send()

        return finish

    def row_weights(d, k):
        z2 = lax.rem(z + d, Z)
        src = vw.at[:, quarter(lax.rem(z2, GS))] if k == 0 else zw
        cols = pl.ds(0, VQ) if k == 0 else pl.ds(VQ, ZH)
        return remote(src, W.at[ctx, :, cols], zsend.at[d - 1, k], zrecv.at[d - 1, k], (y * Z + z2, tp))

    def await_row(d, k):
        src = y * Z + lax.rem(z - d + Z, Z)
        cols = pl.ds(0, VQ) if k == 0 else pl.ds(VQ, ZH)
        ref = W.at[src, :, cols]
        remote(ref, ref, zsend.at[d - 1, k], zrecv.at[d - 1, k], (y * Z + lax.rem(z + d, Z), tp)).wait_recv()

    near = [d for pair in zip(range(1, Z), range(Z - 1, 0, -1)) for d in pair][: Z - 1]
    state = {"slot": 0, "waited": {(0, 0)}}

    def await_piece(oz, oy):
        key = (oz % Z, oy % Y)
        if key in state["waited"]:
            return
        state["waited"].add(key)
        if key[1] == 0:
            await_row(-oz % Z, 0)
            await_row(-oz % Z, 1)
        else:
            src = at(oy, oz)
            remote(W.at[src], W.at[src], wsend.at[0, 0], wrecv.at[src], (at(1, 0), tp)).wait_recv()

    def send_piece(k, i, start):
        oz, oy = plan[k][i]
        src = at(oy, oz)
        c = remote(W.at[src], W.at[src], wsend.at[k, i % DEPTH], wrecv.at[src], (at((1, -1)[k], 0), tp))
        if start:
            c.start()
        else:
            c.wait_send()

    slots = max(len(p) for p in plan)

    def pump(n):
        for _ in range(n):
            i = state["slot"]
            if i >= slots:
                return
            for k in range(2):
                if i < len(plan[k]):
                    await_piece(*plan[k][i])
                    if i >= DEPTH:
                        send_piece(k, i - DEPTH, False)
                    send_piece(k, i, True)
            state["slot"] = i + 1

    def drain():
        pump(slots)
        for k in range(2):
            n = len(plan[k])
            for i in range(max(n - DEPTH, 0), n):
                send_piece(k, i, False)
        for oy in range(Y):
            for oz in range(Z):
                await_piece(oz, oy)
        for d in range(1, Z):
            for k in range(2):
                row_weights(d, k).wait_send()

    stats_row = exchange(0, Z, z, row_peer, S1, S1)
    for d in near:
        for k in range(2):
            row_weights(d, k).start()
    load_v.wait()
    load_z.wait()
    pump(1)
    for c in loads:
        c.wait()

    sine, cosine = sin_cos(phase[...])
    dec = decay[...]
    qr, qi = dec * cosine, dec * sine
    QP[0], QP[1] = qr, qi
    ein = e_in[...]
    QP[2], QP[3] = ein * e_out[0], ein * e_out[1]
    pr, pi = qr, qi
    for k in range(1, 11):
        pr, pi = cmul(pr, pi, pr, pi)
        if k in (4, 5, 6):
            QP[2 * k - 4], QP[2 * k - 3] = pr, pi
        if k == 7:
            q7 = (pr, pi)
        if 2**k == STRETCH * Z:
            q10 = (pr, pi)
    for s in range(Z):
        for n, part in enumerate((*q7, *q10)):
            QX[s, n] = part[s * JS : (s + 1) * JS]
    for t in range(4):
        for j in range(NDIM):
            TB[t, j] = jnp.broadcast_to(QP[t, j : j + 1], (SUB, CL))

    pump(2)
    stats_row()
    before, whole = jnp.zeros((2, CL), f32), jnp.zeros((2, CL), f32)
    for k in range(Z):
        part = S1[k]
        before = before + jnp.where(k < z, part, 0.0)
        whole = whole + part
    S2[y] = whole
    stats_col = exchange(1, Y, y, col_peer, S2, S2)
    pump(4)
    sub_row = lax.broadcasted_iota(jnp.int32, (SUB, LANES), 0)
    stats_col()
    for k in range(Y):
        before = before + jnp.where(k < y, S2[k], 0.0)
    counts = ((ctx * L + lax.broadcasted_iota(jnp.int32, (L, 1), 0)) + 1).astype(f32) * GROUP
    average = (before[0:1] + HID[0]) / counts
    spread = jnp.maximum((before[1:2] + HID[1]) / counts - average * average, 0.0)
    scaled = (tok[...].astype(f32) - average) * lax.rsqrt(spread + 1e-5)
    normed = (scaled * gain[...] + bias[...]).astype(bf16)
    NF[r, tp] = normed
    for t in range(tiles):
        N32[t] = normed[:, t * LANES : (t + 1) * LANES].astype(f32)

    def partner(d):
        low, high = r % 2, r // 2
        return (low + d) % 2 + 2 * ((high + d // 2) % 2)

    def group_peer(d):
        return (y * Z + group * GS + partner(d), tp)

    def group_copy(d, b):
        return remote(NF.at[b, tp], NF.at[b, tp], gsend.at[d - 1], grecv.at[d - 1], group_peer(d))

    def await_group(d):
        group_copy(d, partner(d)).wait_recv()

    group_copy(1, r).start()

    def share(item, plus, ref):
        def hop(block, dev, k):
            return remote(ref(block), ref(block), xsend.at[item, k], xrecv.at[item, k], (ctx, dev))

        sent = []

        def start(c):
            c.start()
            sent.append(c)

        def send():
            if X > 2:
                start(hop(tp, right, 0))
                start(hop(tp, left, 1))
            start(hop(tp, sib, 3))

        def relay():
            if X > 2:
                hop(left, left, 0).wait_recv()
                if plus:
                    start(hop(left, right, 2))
                start(hop(left, sib, 4))
                hop(right, right, 1).wait_recv()
                if not plus:
                    start(hop(right, left, 2))
                start(hop(right, sib, 5))

        def relay_far():
            if X > 2:
                hop(far, right, 2).wait_recv()
                start(hop(far, sib, 6))

        def finish():
            hop(sib, sib, 3).wait_recv()
            if X > 2:
                for k, block in ((4, left), (5, right), (6, far)):
                    hop(block + 1 - 2 * core, sib, k).wait_recv()
            for c in sent:
                c.wait_send()

        return send, relay, relay_far, finish

    def normed_item(i):
        b = partner(i)
        halves = [
            share(2 * i + n, n == 0, lambda block, n=n: NF.at[b, block, pl.ds(n * L // 2, L // 2)]) for n in range(2)
        ]

        def step(k):
            def both():
                for half in halves:
                    half[k]()

            return both

        return [step(k) for k in range(4)]

    normed_items = [normed_item(i) for i in range(GS)]
    mixed_items = [share(2 * GS + t, t < tiles // 2, lambda block, t=t: MF.at[block, t]) for t in range(tiles)]
    normed_items[0][0]()

    per = L // SUB

    def first_pass(t):
        cs = pl.ds(t * LANES, LANES)

        def step(i, st):
            v = N32[t, pl.ds(i, SUB, stride=per)]
            new = []
            for j in range(NDIM):
                sr, si = st[2 * j], st[2 * j + 1]
                a, b = TB[0, j, :, cs], TB[1, j, :, cs]
                new += [a * sr - b * si + v, a * si + b * sr]
            return tuple(new)

        zero = jnp.zeros((SUB, LANES), f32)
        st = lax.fori_loop(0, per, step, (zero,) * (2 * NDIM))
        for j in range(NDIM):
            ir, ii = st[2 * j], st[2 * j + 1]
            for n, sh in enumerate((1, 2, 4)):
                fr, fi = QP[4 + 2 * n, j : j + 1, cs], QP[5 + 2 * n, j : j + 1, cs]
                rr, ri = pltpu.roll(ir, sh, 0), pltpu.roll(ii, sh, 0)
                mr, mi = cmul(fr, fi, rr, ri)
                keep = sub_row >= sh
                ir, ii = ir + jnp.where(keep, mr, 0.0), ii + jnp.where(keep, mi, 0.0)
            TOT[j // JS, j % JS : j % JS + 1, cs] = ir[SUB - 1 : SUB]
            TOT[j // JS, JS + j % JS : JS + j % JS + 1, cs] = ii[SUB - 1 : SUB]
            LOC[j, 0, :, cs] = jnp.where(sub_row >= 1, pltpu.roll(ir, 1, 0), 0.0)
            LOC[j, 1, :, cs] = jnp.where(sub_row >= 1, pltpu.roll(ii, 1, 0), 0.0)

    def sub_powers(t):
        cs = pl.ds(t * LANES, LANES)
        for j in range(NDIM):
            wr, wi = jnp.ones((SUB, LANES), f32), jnp.zeros((SUB, LANES), f32)
            for n, bit in enumerate((1, 2, 4)):
                fr, fi = QP[4 + 2 * n, j : j + 1, cs], QP[5 + 2 * n, j : j + 1, cs]
                mr, mi = cmul(wr, wi, fr, fi)
                on = (sub_row // bit) % 2 == 1
                wr, wi = jnp.where(on, mr, wr), jnp.where(on, mi, wi)
            PW[j, 0, :, cs], PW[j, 1, :, cs] = wr, wi

    for t in range(tiles):
        first_pass(t)
        if t % 2:
            pump(1)

    RS[z] = TOT[z]
    states_row = exchange(2, Z, z, row_peer, TOT, RS)
    for d in range(2, GS):
        group_copy(d, r).start()
    normed_items[0][1]()
    for t in range(tiles):
        sub_powers(t)
    pump(2)
    await_group(1)
    normed_items[1][0]()
    pump(2)
    states_row()
    q128r, q128i, q1kr, q1ki = QX[z, 0], QX[z, 1], QX[z, 2], QX[z, 3]

    def onward(sr, si, fr, fi, part):
        nr, ni = cmul(sr, si, fr, fi)
        return nr + part[0:JS], ni + part[JS : 2 * JS]

    sr, si = jnp.zeros((JS, CL), f32), jnp.zeros((JS, CL), f32)
    for k in range(Z):
        sr, si = onward(sr, si, q128r, q128i, RS[k])
    CS[y, 0:JS], CS[y, JS : 2 * JS] = sr, si
    states_col = exchange(3, Y, y, col_peer, CS, CS)
    pump(2)
    normed_items[0][2]()
    normed_items[1][1]()
    for d in range(2, min(3, GS)):
        await_group(d)
        normed_items[d][0]()
    pump(2)
    states_col()
    sr, si = jnp.zeros((JS, CL), f32), jnp.zeros((JS, CL), f32)
    for k in range(Y):
        nr, ni = onward(sr, si, q1kr, q1ki, CS[k])
        sr, si = jnp.where(k < y, nr, sr), jnp.where(k < y, ni, si)
    for k in range(Z):
        OUTS[k, 0:JS], OUTS[k, JS : 2 * JS] = sr, si
        if k + 1 < Z:
            sr, si = onward(sr, si, q128r, q128i, RS[k])
    IS[z] = OUTS[z]
    states_back = exchange(4, Z, z, row_peer, OUTS, IS)
    pump(2)
    normed_items[1][2]()
    for d in range(3, GS):
        await_group(d)
        normed_items[d][0]()
    for d in range(2, min(3, GS)):
        normed_items[d][1]()
    pump(2)
    states_back()

    def second_pass(t):
        cs = pl.ds(t * LANES, LANES)
        init = []
        for j in range(NDIM):
            gr = IS[j // JS, j % JS : j % JS + 1, cs]
            gi = IS[j // JS, JS + j % JS : JS + j % JS + 1, cs]
            mr, mi = cmul(PW[j, 0, :, cs], PW[j, 1, :, cs], gr, gi)
            init += [LOC[j, 0, :, cs] + mr, LOC[j, 1, :, cs] + mi]
        sk = skip[:, cs]

        def step(i, st):
            v = N32[t, pl.ds(i, SUB, stride=per)]
            new, total = [], sk * v
            for j in range(NDIM):
                sr, si = st[2 * j], st[2 * j + 1]
                a, b = TB[0, j, :, cs], TB[1, j, :, cs]
                nr, ni = a * sr - b * si + v, a * si + b * sr
                total = total + (TB[2, j, :, cs] * nr - TB[3, j, :, cs] * ni)
                new += [nr, ni]
            ACC[t, pl.ds(i, SUB, stride=per)] = total
            return tuple(new)

        lax.fori_loop(0, per, step, tuple(init))

    for t in range(tiles):
        second_pass(t)
        MF[tp, t] = silu(ACC[t]).astype(bf16)
        mixed_items[t][0]()
        if t % 2:
            pump(1)
    for d in range(2, min(3, GS)):
        normed_items[d][2]()
    for d in range(3, GS):
        normed_items[d][1]()
    pump(1)
    for item in mixed_items:
        item[1]()
    for d in range(3, GS):
        normed_items[d][2]()
    pump(2)
    for item in mixed_items:
        item[2]()
    pump(2)
    for item in mixed_items:
        item[3]()

    squares = jnp.zeros((L, LANES), f32)
    for t in range(T):
        for k in range(tiles):
            m = MF[t, k].astype(f32)
            squares = squares + m * m
    rinv = lax.rsqrt(jnp.sum(squares, axis=-1, keepdims=True) * (1.0 / (T * CL)) + 1e-6)
    for t in range(T):
        m = jnp.concatenate([MF[t, k] for k in range(tiles)], axis=1).astype(f32)
        NRM[t] = (m * rinv * rgain[:, t * CL : (t + 1) * CL]).astype(bf16)
    pump(2)
    for item in normed_items:
        item[3]()
    for d in range(1, GS):
        group_copy(d, r).wait_send()

    def weight_rows(t, cols):
        if KR <= CL:
            n = CL // KR
            return W[t * n : (t + 1) * n, :, cols].reshape(CL, -1)
        n = KR // CL
        return W[t // n, (t % n) * CL : (t % n + 1) * CL, cols]

    by_row = T == Y
    if by_row:
        order = [0] + [o for e in range(1, Y // 2 + 1) for o in ((-e, e) if 2 * e < Y else (-e,))]
        for n, oy in enumerate(order):
            if n == len(order) // 2 + 1:
                drain()
            for oz in range(Z):
                await_piece(oz, oy)
            t = lax.rem(y + oy + Y, Y)
            w = W[pl.ds(pl.multiple_of(t * Z, Z), Z), :, 0:VQ].reshape(CL, VQ)
            part = dot(NF[:, t].reshape(GS * L, CL), w)
            VACC[...] = part if n == 0 else VACC[...] + part
    else:
        drain()
        for t in range(T):
            part = dot(NF[:, t].reshape(GS * L, CL), weight_rows(t, slice(0, VQ)))
            VACC[...] = part if t == 0 else VACC[...] + part
    back = []
    for i in (*range(1, GS), 0):
        rows = pl.ds(pl.multiple_of(partner(i) * L, L), L)
        if i == 0:
            VR[r] = silu(VACC[rows]).astype(bf16)
        else:
            VB[i - 1] = silu(VACC[rows]).astype(bf16)
            c = remote(VB.at[i - 1], VR.at[r], vsend.at[i - 1], vrecv.at[i - 1], group_peer(i))
            c.start()
            back.append(c)

    z_total = jnp.zeros((L, ZH), f32)
    for t in range(T):
        z_total = z_total + dot(NRM[t], weight_rows(t, slice(VQ, VQ + ZH)))
    queries = (z_total * affine[0:1] + affine[1:2]).astype(bf16)
    keys = (z_total * affine[2:3] + affine[3:4]).astype(bf16)
    scores = lax.dot_general(
        queries, keys, (((1,), (1,)), ((), ())), preferred_element_type=f32
    ) * (1.0 / ZH**0.5)
    causal = lax.broadcasted_iota(jnp.int32, (L, L), 0) >= lax.broadcasted_iota(jnp.int32, (L, L), 1)
    scores = jnp.where(causal, scores, -1e30)
    weights = jnp.exp(scores - jnp.max(scores, axis=-1, keepdims=True))
    probabilities = (weights / jnp.sum(weights, axis=-1, keepdims=True)).astype(bf16)

    for c in back:
        c.wait()
    for k in range(GS):
        out[:, k * VQ : (k + 1) * VQ] = dot(probabilities, VR[k]).astype(bf16)


def grid_of(mesh):
    n = mesh.shape["ctx"]
    rows = 1
    while rows * rows < n:
        rows *= 2
    return rows, n // rows


def solution(mesh):
    Y, Z = grid_of(mesh)
    T = mesh.shape["tp"]
    X = T // 2
    plan = ring_lists(Y, Z)
    GS = min(4, Z)

    def body(tok, gain, bias, decay, phase, e_in, e_out, skip, rgain, zw, vw, affine):
        L, CL = tok.shape
        KR, VC = vw.shape
        JS = NDIM // Z
        row = lambda a: a.reshape(1, -1)
        vm = pl.BlockSpec(memory_space=pltpu.VMEM)
        hbm = pl.BlockSpec(memory_space=pl.ANY)
        V = pltpu.VMEM
        dma = pltpu.SemaphoreType.DMA
        most = max(Y, Z) - 1
        return pl.pallas_call(
            functools.partial(kernel, Y, Z, X, GS, plan),
            out_shape=jax.ShapeDtypeStruct((L, VC), bf16),
            in_specs=[hbm] * 12,
            out_specs=vm,
            scratch_shapes=[
                V((L, CL), bf16),
                V((1, CL), f32),
                V((1, CL), f32),
                *[V((NDIM, CL), f32)] * 3,
                V((2, NDIM, CL), f32),
                V((1, CL), f32),
                V((1, T * CL), f32),
                V((4, ZH), f32),
                V((Y * Z, KR, VC // GS + ZH), bf16),
                V((GS, T, L, CL), bf16),
                V((T, CL // LANES, L, LANES), bf16),
                V((T, L, CL), bf16),
                V((GS * L, VC // GS), f32),
                V((GS - 1, L, VC // GS), bf16),
                V((GS, L, VC // GS), bf16),
                V((CL // LANES, L, LANES), f32),
                V((4, NDIM, SUB, CL), f32),
                V((NDIM, 2, SUB, CL), f32),
                V((NDIM, 2, SUB, CL), f32),
                V((10, NDIM, CL), f32),
                V((Z, 4, JS, CL), f32),
                V((Z, 2 * JS, CL), f32),
                V((Z, 2 * JS, CL), f32),
                V((Y, 2 * JS, CL), f32),
                V((Z, 2 * JS, CL), f32),
                V((Z, 2 * JS, CL), f32),
                V((Z, 2, CL), f32),
                V((Y, 2, CL), f32),
                V((CL // LANES, L, LANES), f32),
                V((2, L, CL), f32),
                dma((2, DEPTH)),
                dma((Y * Z,)),
                dma((Z - 1, 2)),
                dma((Z - 1, 2)),
                dma((12,)),
                dma((5, most)),
                dma((5, most)),
                dma((2 * GS + CL // LANES, 7)),
                dma((2 * GS + CL // LANES, 7)),
                dma((GS - 1,)),
                dma((GS - 1,)),
                dma((GS - 1,)),
                dma((GS - 1,)),
            ],
            compiler_params=pltpu.CompilerParams(
                collective_id=0, has_side_effects=True, vmem_limit_bytes=60 << 20
            ),
        )(tok, row(gain), row(bias), decay, phase, e_in, e_out, row(skip), row(rgain), zw, vw, affine)

    in_specs = (
        P("ctx", "tp"), P("tp"), P("tp"), P(None, "tp"), P(None, "tp"), P(None, "tp"), P(None, None, "tp"),
        P("tp"), P(), P("ctx", "tp"), P("ctx", "tp"), P(None, "tp"),
    )
    return jax.shard_map(body, mesh=mesh, in_specs=in_specs, out_specs=P("ctx", "tp"), check_vma=False)
```

```python
import functools
import math

import jax
import jax.numpy as jnp
from jax import lax
from jax.experimental import pallas as pl
from jax.experimental.pallas import tpu as pltpu
from jax.sharding import PartitionSpec as P

NDIM = 16
ZH = 128
GROUP = 64
STRETCH = 128
SUB = 8
LANES = 128
DEPTH = 4
MESH = pl.DeviceIdType.MESH
f32 = jnp.float32
bf16 = jnp.bfloat16
highest = lax.Precision.HIGHEST


def ring_lists(Y, Z):
    columns = [0]
    for d in range(1, Z // 2 + 1):
        columns += [-d] if 2 * d == Z else [-d, d]
    plus, minus = [], []
    for e in range(Y // 2 + 1):
        for i, oz in enumerate(columns):
            more, less = Y // 2, (Y - 1) // 2
            if e < (less if i % 2 else more):
                plus.append((oz, -e))
            if e < (more if i % 2 else less):
                minus.append((oz, e))
    return plus, minus


def silu(v):
    return v * (1.0 / (1.0 + jnp.exp(-v)))


def cmul(ar, ai, br, bi):
    return ar * br - ai * bi, ar * bi + ai * br


def sin_cos(p):
    s = p * p
    sine = p * (1.0 + s * (-1 / 6 + s * (1 / 120 + s * (-1 / 5040 + s * (1 / 362880 - s / 39916800)))))
    cosine = 1.0 + s * (
        -0.5 + s * (1 / 24 + s * (-1 / 720 + s * (1 / 40320 + s * (-1 / 3628800 + s / 479001600))))
    )
    return sine, cosine


def kernel(
    Y, Z, X, GS, plan,
    tok_h, gain_h, bias_h, decay_h, phase_h, e_in_h, e_out_h, skip_h, rgain_h, zw, vw, affine_h,
    out,
    tok, gain, bias, decay, phase, e_in, e_out, skip, rgain, affine,
    W, NF, MF, NRM, VACC, VB, VR, N32, TB, LOC, PW, QP, QX, TOT, RS, CS, OUTS, IS, S1, S2, ACC, HID,
    wsend, wrecv, zsend, zrecv, lsem, ssend, srecv, xsend, xrecv, gsend, grecv, vsend, vrecv,
):
    ctx, tp = lax.axis_index("ctx"), lax.axis_index("tp")
    y, z = ctx // Z, ctx % Z
    x, core = tp // 2, tp % 2
    group, r = z // GS, z % GS
    _, T, L, CL = NF.shape
    KR = W.shape[1]
    VC = vw.shape[1]
    VQ = VC // GS
    JS = NDIM // Z
    tiles = CL // LANES
    sib = x * 2 + (1 - core)
    right, left, far = (lax.rem(x + d, X) * 2 + core for d in (1, X - 1, X // 2))

    def at(dy, dz):
        return lax.rem(y + dy + Y, Y) * Z + lax.rem(z + dz + Z, Z)

    def remote(src, dst, send, recv, dev):
        return pltpu.make_async_remote_copy(
            src_ref=src, dst_ref=dst, send_sem=send, recv_sem=recv, device_id=dev, device_id_type=MESH
        )

    barrier = pltpu.get_barrier_semaphore()
    peers = [(y * Z + lax.rem(z + d, Z), tp) for d in range(1, Z)]
    peers += [(lax.rem(y + d, Y) * Z + z, tp) for d in range(1, Y)]
    peers += [(ctx, right), (ctx, left)] if X > 2 else []
    peers += [(ctx, sib)]
    for peer in peers:
        pl.semaphore_signal(barrier, inc=1, device_id=peer, device_id_type=MESH)

    def quarter(k):
        return pl.ds(pl.multiple_of(k * VQ, VQ), VQ)

    load_tok = pltpu.make_async_copy(tok_h, tok, lsem.at[2])
    load_tok.start()
    load_v = pltpu.make_async_copy(vw.at[:, quarter(r)], W.at[ctx, :, pl.ds(0, VQ)], lsem.at[0])
    load_z = pltpu.make_async_copy(zw, W.at[ctx, :, pl.ds(VQ, ZH)], lsem.at[1])
    load_v.start()
    load_z.start()
    small = (
        (decay_h, decay), (phase_h, phase), (e_in_h, e_in), (e_out_h, e_out), (gain_h, gain), (bias_h, bias),
        (skip_h, skip), (rgain_h, rgain), (affine_h, affine),
    )
    loads = [pltpu.make_async_copy(a, b, lsem.at[3 + k]) for k, (a, b) in enumerate(small)]
    for c in loads:
        c.start()

    load_tok.wait()
    xb = tok[...]
    xf = xb.astype(f32)
    same = (
        lax.broadcasted_iota(jnp.int32, (CL, CL), 0) // GROUP
        == lax.broadcasted_iota(jnp.int32, (CL, CL), 1) // GROUP
    )
    same = jnp.where(same, 1.0, 0.0).astype(bf16)
    sq = xf * xf
    sq_hi = sq.astype(bf16)
    sq_lo = (sq - sq_hi.astype(f32)).astype(bf16)
    dot = functools.partial(jnp.dot, preferred_element_type=f32)
    row_sums = dot(xb, same)
    row_squares = dot(sq_hi, same) + dot(sq_lo, same)
    lower = jnp.where(
        lax.broadcasted_iota(jnp.int32, (L, L), 0) >= lax.broadcasted_iota(jnp.int32, (L, L), 1), 1.0, 0.0
    ).astype(f32)
    run_sums = dot(lower, row_sums, precision=highest)
    run_squares = dot(lower, row_squares, precision=highest)
    HID[0] = run_sums
    HID[1] = run_squares
    S1[z, 0:1] = run_sums[L - 1 : L]
    S1[z, 1:2] = run_squares[L - 1 : L]

    pl.semaphore_wait(barrier, len(peers))

    def row_peer(d):
        z2 = lax.rem(z + d, Z)
        return z2, (y * Z + z2, tp)

    def col_peer(d):
        y2 = lax.rem(y + d, Y)
        return y2, (y2 * Z + z, tp)

    def exchange(phase_at, n, mine, peer_of, source, dest):
        copies = []
        for d in range(1, n):
            who, dev = peer_of(d)
            c = pltpu.make_async_remote_copy(
                src_ref=source.at[who] if source is not dest else source.at[mine],
                dst_ref=dest.at[mine],
                send_sem=ssend.at[phase_at, d - 1],
                recv_sem=srecv.at[phase_at, d - 1],
                device_id=dev,
                device_id_type=MESH,
            )
            c.start()
            copies.append(c)

        def finish():
            for c in copies:
                c.wait_recv()
            for c in copies:
                c.wait_send()

        return finish

    def row_weights(d, k):
        z2 = lax.rem(z + d, Z)
        src = vw.at[:, quarter(lax.rem(z2, GS))] if k == 0 else zw
        cols = pl.ds(0, VQ) if k == 0 else pl.ds(VQ, ZH)
        return remote(src, W.at[ctx, :, cols], zsend.at[d - 1, k], zrecv.at[d - 1, k], (y * Z + z2, tp))

    def await_row(d, k):
        src = y * Z + lax.rem(z - d + Z, Z)
        cols = pl.ds(0, VQ) if k == 0 else pl.ds(VQ, ZH)
        ref = W.at[src, :, cols]
        remote(ref, ref, zsend.at[d - 1, k], zrecv.at[d - 1, k], (y * Z + lax.rem(z + d, Z), tp)).wait_recv()

    near = [d for pair in zip(range(1, Z), range(Z - 1, 0, -1)) for d in pair][: Z - 1]
    state = {"slot": 0, "waited": {(0, 0)}}

    def await_piece(oz, oy):
        key = (oz % Z, oy % Y)
        if key in state["waited"]:
            return
        state["waited"].add(key)
        if key[1] == 0:
            await_row(-oz % Z, 0)
            await_row(-oz % Z, 1)
        else:
            src = at(oy, oz)
            remote(W.at[src], W.at[src], wsend.at[0, 0], wrecv.at[src], (at(1, 0), tp)).wait_recv()

    def send_piece(k, i, start):
        oz, oy = plan[k][i]
        src = at(oy, oz)
        c = remote(W.at[src], W.at[src], wsend.at[k, i % DEPTH], wrecv.at[src], (at((1, -1)[k], 0), tp))
        if start:
            c.start()
        else:
            c.wait_send()

    slots = max(len(p) for p in plan)

    def pump(n):
        for _ in range(n):
            i = state["slot"]
            if i >= slots:
                return
            for k in range(2):
                if i < len(plan[k]):
                    await_piece(*plan[k][i])
                    if i >= DEPTH:
                        send_piece(k, i - DEPTH, False)
                    send_piece(k, i, True)
            state["slot"] = i + 1

    def drain():
        pump(slots)
        for k in range(2):
            n = len(plan[k])
            for i in range(max(n - DEPTH, 0), n):
                send_piece(k, i, False)
        for oy in range(Y):
            for oz in range(Z):
                await_piece(oz, oy)
        for d in range(1, Z):
            for k in range(2):
                row_weights(d, k).wait_send()

    stats_row = exchange(0, Z, z, row_peer, S1, S1)
    for d in near:
        for k in range(2):
            row_weights(d, k).start()
    load_v.wait()
    load_z.wait()
    pump(1)
    for c in loads:
        c.wait()

    sine, cosine = sin_cos(phase[...])
    dec = decay[...]
    qr, qi = dec * cosine, dec * sine
    QP[0], QP[1] = qr, qi
    ein = e_in[...]
    QP[2], QP[3] = ein * e_out[0], ein * e_out[1]
    pr, pi = qr, qi
    for k in range(1, 11):
        pr, pi = cmul(pr, pi, pr, pi)
        if k in (4, 5, 6):
            QP[2 * k - 4], QP[2 * k - 3] = pr, pi
        if k == 7:
            q7 = (pr, pi)
        if 2**k == STRETCH * Z:
            q10 = (pr, pi)
    for s in range(Z):
        for n, part in enumerate((*q7, *q10)):
            QX[s, n] = part[s * JS : (s + 1) * JS]
    for t in range(4):
        for j in range(NDIM):
            TB[t, j] = jnp.broadcast_to(QP[t, j : j + 1], (SUB, CL))

    pump(2)
    stats_row()
    before, whole = jnp.zeros((2, CL), f32), jnp.zeros((2, CL), f32)
    for k in range(Z):
        part = S1[k]
        before = before + jnp.where(k < z, part, 0.0)
        whole = whole + part
    S2[y] = whole
    stats_col = exchange(1, Y, y, col_peer, S2, S2)
    pump(4)
    sub_row = lax.broadcasted_iota(jnp.int32, (SUB, LANES), 0)
    stats_col()
    for k in range(Y):
        before = before + jnp.where(k < y, S2[k], 0.0)
    counts = ((ctx * L + lax.broadcasted_iota(jnp.int32, (L, 1), 0)) + 1).astype(f32) * GROUP
    average = (before[0:1] + HID[0]) / counts
    spread = jnp.maximum((before[1:2] + HID[1]) / counts - average * average, 0.0)
    scaled = (tok[...].astype(f32) - average) * lax.rsqrt(spread + 1e-5)
    normed = (scaled * gain[...] + bias[...]).astype(bf16)
    NF[r, tp] = normed
    for t in range(tiles):
        N32[t] = normed[:, t * LANES : (t + 1) * LANES].astype(f32)

    def partner(d):
        low, high = r % 2, r // 2
        return (low + d) % 2 + 2 * ((high + d // 2) % 2)

    def group_peer(d):
        return (y * Z + group * GS + partner(d), tp)

    def group_copy(d, b):
        return remote(NF.at[b, tp], NF.at[b, tp], gsend.at[d - 1], grecv.at[d - 1], group_peer(d))

    def await_group(d):
        group_copy(d, partner(d)).wait_recv()

    group_copy(1, r).start()

    def share(item, plus, ref):
        def hop(block, dev, k):
            return remote(ref(block), ref(block), xsend.at[item, k], xrecv.at[item, k], (ctx, dev))

        sent = []

        def start(c):
            c.start()
            sent.append(c)

        def send():
            if X > 2:
                start(hop(tp, right, 0))
                start(hop(tp, left, 1))
            start(hop(tp, sib, 3))

        def relay():
            if X > 2:
                hop(left, left, 0).wait_recv()
                if plus:
                    start(hop(left, right, 2))
                start(hop(left, sib, 4))
                hop(right, right, 1).wait_recv()
                if not plus:
                    start(hop(right, left, 2))
                start(hop(right, sib, 5))

        def relay_far():
            if X > 2:
                hop(far, right, 2).wait_recv()
                start(hop(far, sib, 6))

        def finish():
            hop(sib, sib, 3).wait_recv()
            if X > 2:
                for k, block in ((4, left), (5, right), (6, far)):
                    hop(block + 1 - 2 * core, sib, k).wait_recv()
            for c in sent:
                c.wait_send()

        return send, relay, relay_far, finish

    def normed_item(i):
        b = partner(i)
        halves = [
            share(2 * i + n, n == 0, lambda block, n=n: NF.at[b, block, pl.ds(n * L // 2, L // 2)]) for n in range(2)
        ]

        def step(k):
            def both():
                for half in halves:
                    half[k]()

            return both

        return [step(k) for k in range(4)]

    normed_items = [normed_item(i) for i in range(GS)]
    mixed_items = [share(2 * GS + t, t < tiles // 2, lambda block, t=t: MF.at[block, t]) for t in range(tiles)]
    normed_items[0][0]()

    per = L // SUB

    def first_pass(t):
        cs = pl.ds(t * LANES, LANES)

        def step(i, st):
            v = N32[t, pl.ds(i, SUB, stride=per)]
            new = []
            for j in range(NDIM):
                sr, si = st[2 * j], st[2 * j + 1]
                a, b = TB[0, j, :, cs], TB[1, j, :, cs]
                new += [a * sr - b * si + v, a * si + b * sr]
            return tuple(new)

        zero = jnp.zeros((SUB, LANES), f32)
        st = lax.fori_loop(0, per, step, (zero,) * (2 * NDIM))
        for j in range(NDIM):
            ir, ii = st[2 * j], st[2 * j + 1]
            for n, sh in enumerate((1, 2, 4)):
                fr, fi = QP[4 + 2 * n, j : j + 1, cs], QP[5 + 2 * n, j : j + 1, cs]
                rr, ri = pltpu.roll(ir, sh, 0), pltpu.roll(ii, sh, 0)
                mr, mi = cmul(fr, fi, rr, ri)
                keep = sub_row >= sh
                ir, ii = ir + jnp.where(keep, mr, 0.0), ii + jnp.where(keep, mi, 0.0)
            TOT[j // JS, j % JS : j % JS + 1, cs] = ir[SUB - 1 : SUB]
            TOT[j // JS, JS + j % JS : JS + j % JS + 1, cs] = ii[SUB - 1 : SUB]
            LOC[j, 0, :, cs] = jnp.where(sub_row >= 1, pltpu.roll(ir, 1, 0), 0.0)
            LOC[j, 1, :, cs] = jnp.where(sub_row >= 1, pltpu.roll(ii, 1, 0), 0.0)

    def sub_powers(t):
        cs = pl.ds(t * LANES, LANES)
        for j in range(NDIM):
            wr, wi = jnp.ones((SUB, LANES), f32), jnp.zeros((SUB, LANES), f32)
            for n, bit in enumerate((1, 2, 4)):
                fr, fi = QP[4 + 2 * n, j : j + 1, cs], QP[5 + 2 * n, j : j + 1, cs]
                mr, mi = cmul(wr, wi, fr, fi)
                on = (sub_row // bit) % 2 == 1
                wr, wi = jnp.where(on, mr, wr), jnp.where(on, mi, wi)
            PW[j, 0, :, cs], PW[j, 1, :, cs] = wr, wi

    for t in range(tiles):
        first_pass(t)
        if t % 2:
            pump(1)

    RS[z] = TOT[z]
    states_row = exchange(2, Z, z, row_peer, TOT, RS)
    for d in range(2, GS):
        group_copy(d, r).start()
    for t in range(tiles):
        sub_powers(t)
    pump(2)
    normed_items[0][1]()
    await_group(1)
    normed_items[1][0]()
    pump(2)
    states_row()
    q128r, q128i, q1kr, q1ki = QX[z, 0], QX[z, 1], QX[z, 2], QX[z, 3]

    def onward(sr, si, fr, fi, part):
        nr, ni = cmul(sr, si, fr, fi)
        return nr + part[0:JS], ni + part[JS : 2 * JS]

    sr, si = jnp.zeros((JS, CL), f32), jnp.zeros((JS, CL), f32)
    for k in range(Z):
        sr, si = onward(sr, si, q128r, q128i, RS[k])
    CS[y, 0:JS], CS[y, JS : 2 * JS] = sr, si
    states_col = exchange(3, Y, y, col_peer, CS, CS)
    pump(2)
    normed_items[0][2]()
    normed_items[1][1]()
    for d in range(2, min(3, GS)):
        await_group(d)
        normed_items[d][0]()
    pump(2)
    states_col()
    sr, si = jnp.zeros((JS, CL), f32), jnp.zeros((JS, CL), f32)
    for k in range(Y):
        nr, ni = onward(sr, si, q1kr, q1ki, CS[k])
        sr, si = jnp.where(k < y, nr, sr), jnp.where(k < y, ni, si)
    for k in range(Z):
        OUTS[k, 0:JS], OUTS[k, JS : 2 * JS] = sr, si
        if k + 1 < Z:
            sr, si = onward(sr, si, q128r, q128i, RS[k])
    IS[z] = OUTS[z]
    states_back = exchange(4, Z, z, row_peer, OUTS, IS)
    pump(2)
    normed_items[1][2]()
    for d in range(3, GS):
        await_group(d)
        normed_items[d][0]()
    for d in range(2, min(3, GS)):
        normed_items[d][1]()
    pump(2)
    states_back()

    def second_pass(t):
        cs = pl.ds(t * LANES, LANES)
        init = []
        for j in range(NDIM):
            gr = IS[j // JS, j % JS : j % JS + 1, cs]
            gi = IS[j // JS, JS + j % JS : JS + j % JS + 1, cs]
            mr, mi = cmul(PW[j, 0, :, cs], PW[j, 1, :, cs], gr, gi)
            init += [LOC[j, 0, :, cs] + mr, LOC[j, 1, :, cs] + mi]
        sk = skip[:, cs]

        def step(i, st):
            v = N32[t, pl.ds(i, SUB, stride=per)]
            new, total = [], sk * v
            for j in range(NDIM):
                sr, si = st[2 * j], st[2 * j + 1]
                a, b = TB[0, j, :, cs], TB[1, j, :, cs]
                nr, ni = a * sr - b * si + v, a * si + b * sr
                total = total + (TB[2, j, :, cs] * nr - TB[3, j, :, cs] * ni)
                new += [nr, ni]
            ACC[t, pl.ds(i, SUB, stride=per)] = total
            return tuple(new)

        lax.fori_loop(0, per, step, tuple(init))

    for t in range(tiles):
        second_pass(t)
        MF[tp, t] = silu(ACC[t]).astype(bf16)
        mixed_items[t][0]()
        if t % 2:
            pump(1)
    for d in range(2, min(3, GS)):
        normed_items[d][2]()
    for d in range(3, GS):
        normed_items[d][1]()
    pump(1)
    for item in mixed_items:
        item[1]()
    for d in range(3, GS):
        normed_items[d][2]()
    pump(2)
    pump(2)
    pump(2)
    for item in normed_items:
        item[3]()
    for d in range(1, GS):
        group_copy(d, r).wait_send()

    def weight_rows(t, cols):
        if KR <= CL:
            n = CL // KR
            return W[t * n : (t + 1) * n, :, cols].reshape(CL, -1)
        n = KR // CL
        return W[t // n, (t % n) * CL : (t % n + 1) * CL, cols]

    by_row = T == Y
    if by_row:
        order = [0] + [o for e in range(1, Y // 2 + 1) for o in ((-e, e) if 2 * e < Y else (-e,))]
        for n, oy in enumerate(order):
            if n == len(order) // 2 + 1:
                drain()
            for oz in range(Z):
                await_piece(oz, oy)
            t = lax.rem(y + oy + Y, Y)
            w = W[pl.ds(pl.multiple_of(t * Z, Z), Z), :, 0:VQ].reshape(CL, VQ)
            part = dot(NF[:, t].reshape(GS * L, CL), w)
            VACC[...] = part if n == 0 else VACC[...] + part
    else:
        drain()
        for t in range(T):
            part = dot(NF[:, t].reshape(GS * L, CL), weight_rows(t, slice(0, VQ)))
            VACC[...] = part if t == 0 else VACC[...] + part
    back = []
    for i in (*range(1, GS), 0):
        rows = pl.ds(pl.multiple_of(partner(i) * L, L), L)
        if i == 0:
            VR[r] = silu(VACC[rows]).astype(bf16)
        else:
            VB[i - 1] = silu(VACC[rows]).astype(bf16)
            c = remote(VB.at[i - 1], VR.at[r], vsend.at[i - 1], vrecv.at[i - 1], group_peer(i))
            c.start()
            back.append(c)

    for item in mixed_items:
        item[2]()
    for item in mixed_items:
        item[3]()

    squares = jnp.zeros((L, LANES), f32)
    for t in range(T):
        for k in range(tiles):
            m = MF[t, k].astype(f32)
            squares = squares + m * m
    rinv = lax.rsqrt(jnp.sum(squares, axis=-1, keepdims=True) * (1.0 / (T * CL)) + 1e-6)
    for t in range(T):
        m = jnp.concatenate([MF[t, k] for k in range(tiles)], axis=1).astype(f32)
        NRM[t] = (m * rinv * rgain[:, t * CL : (t + 1) * CL]).astype(bf16)
    z_total = jnp.zeros((L, ZH), f32)
    for t in range(T):
        z_total = z_total + dot(NRM[t], weight_rows(t, slice(VQ, VQ + ZH)))
    queries = (z_total * affine[0:1] + affine[1:2]).astype(bf16)
    keys = (z_total * affine[2:3] + affine[3:4]).astype(bf16)
    scores = lax.dot_general(
        queries, keys, (((1,), (1,)), ((), ())), preferred_element_type=f32
    ) * (1.0 / ZH**0.5)
    causal = lax.broadcasted_iota(jnp.int32, (L, L), 0) >= lax.broadcasted_iota(jnp.int32, (L, L), 1)
    scores = jnp.where(causal, scores, -1e30)
    weights = jnp.exp(scores - jnp.max(scores, axis=-1, keepdims=True))
    probabilities = (weights / jnp.sum(weights, axis=-1, keepdims=True)).astype(bf16)

    for c in back:
        c.wait()
    for k in range(GS):
        out[:, k * VQ : (k + 1) * VQ] = dot(probabilities, VR[k]).astype(bf16)


def grid_of(mesh):
    n = mesh.shape["ctx"]
    rows = 1
    while rows * rows < n:
        rows *= 2
    return rows, n // rows


def solution(mesh):
    Y, Z = grid_of(mesh)
    T = mesh.shape["tp"]
    X = T // 2
    plan = ring_lists(Y, Z)
    GS = min(4, Z)

    def body(tok, gain, bias, decay, phase, e_in, e_out, skip, rgain, zw, vw, affine):
        L, CL = tok.shape
        KR, VC = vw.shape
        JS = NDIM // Z
        row = lambda a: a.reshape(1, -1)
        vm = pl.BlockSpec(memory_space=pltpu.VMEM)
        hbm = pl.BlockSpec(memory_space=pl.ANY)
        V = pltpu.VMEM
        dma = pltpu.SemaphoreType.DMA
        most = max(Y, Z) - 1
        return pl.pallas_call(
            functools.partial(kernel, Y, Z, X, GS, plan),
            out_shape=jax.ShapeDtypeStruct((L, VC), bf16),
            in_specs=[hbm] * 12,
            out_specs=vm,
            scratch_shapes=[
                V((L, CL), bf16),
                V((1, CL), f32),
                V((1, CL), f32),
                *[V((NDIM, CL), f32)] * 3,
                V((2, NDIM, CL), f32),
                V((1, CL), f32),
                V((1, T * CL), f32),
                V((4, ZH), f32),
                V((Y * Z, KR, VC // GS + ZH), bf16),
                V((GS, T, L, CL), bf16),
                V((T, CL // LANES, L, LANES), bf16),
                V((T, L, CL), bf16),
                V((GS * L, VC // GS), f32),
                V((GS - 1, L, VC // GS), bf16),
                V((GS, L, VC // GS), bf16),
                V((CL // LANES, L, LANES), f32),
                V((4, NDIM, SUB, CL), f32),
                V((NDIM, 2, SUB, CL), f32),
                V((NDIM, 2, SUB, CL), f32),
                V((10, NDIM, CL), f32),
                V((Z, 4, JS, CL), f32),
                V((Z, 2 * JS, CL), f32),
                V((Z, 2 * JS, CL), f32),
                V((Y, 2 * JS, CL), f32),
                V((Z, 2 * JS, CL), f32),
                V((Z, 2 * JS, CL), f32),
                V((Z, 2, CL), f32),
                V((Y, 2, CL), f32),
                V((CL // LANES, L, LANES), f32),
                V((2, L, CL), f32),
                dma((2, DEPTH)),
                dma((Y * Z,)),
                dma((Z - 1, 2)),
                dma((Z - 1, 2)),
                dma((12,)),
                dma((5, most)),
                dma((5, most)),
                dma((2 * GS + CL // LANES, 7)),
                dma((2 * GS + CL // LANES, 7)),
                dma((GS - 1,)),
                dma((GS - 1,)),
                dma((GS - 1,)),
                dma((GS - 1,)),
            ],
            compiler_params=pltpu.CompilerParams(
                collective_id=0, has_side_effects=True, vmem_limit_bytes=60 << 20
            ),
        )(tok, row(gain), row(bias), decay, phase, e_in, e_out, row(skip), row(rgain), zw, vw, affine)

    in_specs = (
        P("ctx", "tp"), P("tp"), P("tp"), P(None, "tp"), P(None, "tp"), P(None, "tp"), P(None, None, "tp"),
        P("tp"), P(), P("ctx", "tp"), P("ctx", "tp"), P(None, "tp"),
    )
    return jax.shard_map(body, mesh=mesh, in_specs=in_specs, out_specs=P("ctx", "tp"), check_vma=False)
```
